128 devices in a mesh: seq: 8 (over x_lo, z), exp: 16 (over x_hi, y, core).
Axes of the slice: x: 4 (x_hi: 2, x_lo: 2; x = x_hi * 2 + x_lo), y: 4, z: 4, core: 2. Of those that a mesh axis runs over, the one named last changes fastest.
Arguments:
- tokens: bfloat16 [16, 1024, 2048], P('exp', 'seq'), may hold values from -6 to 6
- position_of_row: int32 [16, 1024], P('exp'), may hold values from 0 to 1023, each once within a row
- request_of_position: int32 [16, 1024], P('exp'), may hold values from 0 to 3, never falling along the last dimension, each value on 1 to 512 neighbouring positions
- expert_ids: int32 [16, 1024, 6], P('exp', 'seq'), may hold values from 0 to 63, all different within a row; in each aligned block of 128 rows (0 to 127, 128 to 255, ..., all dimensions but the last counted through in order) at most 16 rows name the same one
- gate_values: float32 [16, 1024, 6], P('exp', 'seq'), may hold values from 0.1 to 1
- attn_norm: bfloat16 [2048], replicated, may hold values from 0.25 to 1.75
- moe_norm: bfloat16 [2048], replicated, may hold values from 0.25 to 1.75
- w_query: bfloat16 [2048, 2048], P(None, 'seq'), may hold values from -0.125 to 0.125
- w_latent: bfloat16 [2048, 512], replicated, may hold values from -0.125 to 0.125
- w_key_up: bfloat16 [512, 2048], P(None, 'seq'), may hold values from -120 to 120
- w_value_up: bfloat16 [512, 2048], P(None, 'seq'), may hold values from -0.25 to 0.25
- w_output: bfloat16 [2048, 2048], P('seq'), may hold values from -0.125 to 0.125
- w_shared_gate: bfloat16 [2048, 2816], P(None, 'seq'), may hold values from -0.125 to 0.125
- w_shared_up: bfloat16 [2048, 2816], P(None, 'seq'), may hold values from -0.125 to 0.125
- w_shared_down: bfloat16 [2816, 2048], P('seq'), may hold values from -0.109375 to 0.109375
- w_routed_gate: bfloat16 [128, 2048, 704], P(('seq', 'exp')), may hold values from -0.125 to 0.125
- w_routed_up: bfloat16 [128, 2048, 704], P(('seq', 'exp')), may hold values from -0.125 to 0.125
- w_routed_down: bfloat16 [128, 704, 2048], P(('seq', 'exp')), may hold values from -0.15625 to 0.15625
Outputs:
- layer_out: bfloat16 [16, 1024, 2048], P('exp', 'seq')
The draws below stay inside these ranges and needn't reach their ends.
Inputs may be any that keep to these rules, and one draw needn't show every extreme that they name: `expert_ids`: each row names 6 different experts; among the rows of one device no expert is named by more than 16 rows, and some expert reaches 16 on some device. `position_of_row`: each row of a group holds a different position. `request_of_position`: never falls along positions; each request holds 1 to 512 positions.
All inputs are finite; a program needn't handle non-finite values.
Results may differ from the reference program's by a relative error of at most 0.027.
The reference program's roundings to bfloat16 on the way count: a program that leaves them out, or rounds other values in their place, can miss the bound.
Values may be sent and summed in bfloat16 or wider, within the bound.
No kernel may reach another device: no remote copies, remote signals or barrier semaphores. Data moves between devices by JAX's collectives and lax.ppermute only.
A program may use at most 128 MiB of HBM per device.

```python
import math
import jax
import jax.numpy as jnp
import numpy as np
from jax import lax

D = 2048
HEADS = 16
HD = 128
LAT = 512
FF = 1408
SHARED_FF = 2816
TOP = 6
TOK_DEV = 128
REQS = 4
FFH = 704
EXPERTS = 64
HALVES = 128
CAP = 16
GROUPS = 16
GROUP_TOK = 1024
MOST_REQ = 512
DEVICES = 128


def draw_w_key_up(key, part):
    base_key = jax.random.fold_in(key, 11)
    values = jax.random.truncated_normal(base_key, -4.0, 4.0, (LAT, HEADS * HD), jnp.float32) * HD ** (-0.5)
    return values.astype(jnp.bfloat16)


def level_of(rng, dims, shards, smallest, top_value):
    level, own = 1.0, jax.random.fold_in(rng, 6)
    for position, shards_of in shards:
        heights = jnp.exp(jax.random.uniform(jax.random.fold_in(own, position), (shards_of,), jnp.float32, smallest / len(shards), top_value / len(shards)))
        level = level * jnp.repeat(heights, dims[position] // shards_of).reshape([-1 if axis == position else 1 for axis in range(len(dims))])
    return level


def length_profile(count, total, reach, skew):
    weights = [(1 << 20) // math.isqrt(grade ** skew) + 1 for grade in range(2, count + 1)]
    spare, holding = total - reach - (count - 1), [1] * (count - 1)
    while spare > 0:
        free = [i for i in range(count - 1) if holding[i] < reach]
        mass, left = sum([weights[i] for i in free]), spare
        for i in free:
            addition = min(reach - holding[i], max(1, left * weights[i] // mass), spare)
            holding[i] = holding[i] + addition
            spare = spare - addition
    return np.array([reach] + holding)


def uneven_parts(rng, amount, total, bound, slope):
    if amount == 2:
        one = jax.random.randint(rng, (), max(1, total - bound), min(bound, total - 1) + 1)
        return jnp.stack([one, total - one])
    sizes = jnp.asarray(length_profile(amount, total, bound, slope), jnp.int32)
    pairs = (amount - 1) // 2
    giver, taker = sizes[1:1 + 2 * pairs:2], sizes[2:2 + 2 * pairs:2]
    margin = jnp.minimum(giver - 1, bound - taker)
    shifted = jax.random.randint(jax.random.fold_in(rng, 1), (pairs,), 0, 1 << 20) % (margin + 1)
    sizes = sizes.at[1:1 + 2 * pairs:2].set(giver - shifted).at[2:2 + 2 * pairs:2].set(taker + shifted)
    return sizes[jax.random.permutation(jax.random.fold_in(rng, 2), amount)]


def routed_block(stream_key, own, number, rows, count, top, reach, slope):
    sequence = jax.random.permutation(stream_key, count)
    crowded, common = shares(count, rows * top, reach, slope, True), shares(count, rows * top, reach, slope, False)
    places = jnp.arange(count)

    def named(lengths, rotation):
        used = int((lengths > 0).sum())
        fixed = max(1, used // 4)
        moved = fixed + (places - fixed + rotation * (used - fixed)) % max(1, count - fixed)
        return jnp.zeros((count,), jnp.int32).at[sequence[jnp.where(places < fixed, places, moved)]].set(jnp.asarray(lengths, jnp.int32))

    lengths = jnp.where(number % 4 == 0, named(crowded, number // 4), named(common, number - number // 4 - 1))
    mixed = jax.random.permutation(jax.random.fold_in(own, 3), count)
    giver, taker = mixed[0:count // 2 * 2:2], mixed[1:count // 2 * 2:2]
    room = jnp.minimum(lengths[giver] - 1, reach - lengths[taker]) // 2
    room = jnp.where((giver == sequence[0]) | (taker == sequence[0]) | (lengths[taker] == 0), 0, jnp.maximum(room, 0))
    moved = jax.random.randint(jax.random.fold_in(own, 4), (count // 2,), 0, 1 << 20) % (room + 1)
    lengths = lengths.at[giver].add(-moved).at[taker].add(moved)
    members = jnp.searchsorted(jnp.cumsum(lengths), jnp.arange(rows * top), side="right").astype(jnp.int32)
    table = members.reshape(top, rows).T
    table = table[jax.random.permutation(jax.random.fold_in(own, 1), rows)]
    rotation = jax.random.randint(jax.random.fold_in(own, 2), (rows, 1), 0, top)
    return jnp.take_along_axis(table, (jnp.arange(top)[None, :] + rotation) % top, axis=1)


def shares(amount, total, bound, skew, full):
    loads = [(1 << 20) // math.isqrt(rank ** skew) + 1 for rank in range(1, amount + 1)]
    largest = bound if full else min(bound, max(-(-total // amount), total * loads[0] // sum(loads)))
    least = 1 if total - largest >= amount - 1 else 0
    holding, rest = [largest] + [least] * (amount - 1), total - largest - least * (amount - 1)
    while rest > 0:
        candidates = [i for i in range(1, amount) if holding[i] < largest] or [i for i in range(1, amount) if holding[i] < bound]
        mass, remaining = sum([loads[i] for i in candidates]), rest
        for i in candidates:
            extra = min(bound - holding[i], max(1, remaining * loads[i] // mass), rest)
            holding[i] = holding[i] + extra
            rest = rest - extra
    return np.array(holding)


def gaussian(key, shape, deviation, most, split=(), kind=jnp.bfloat16):
    values = deviation * jax.random.normal(key, shape, jnp.float32)
    if split:
        values = values * level_of(key, shape, split, -0.22, 0.18)
    return jnp.clip(values, -most, most).astype(kind)


def setup_inputs(seed: int = 0) -> dict:
    splits = jax.random.split(jax.random.key(seed), 19)
    tokens = gaussian(splits[0], (GROUPS, GROUP_TOK, D), 1.0, 6.0, ((0, 16), (1, 8)))
    position_of_row = jax.vmap(lambda own: jax.random.permutation(own, GROUP_TOK))(jax.random.split(splits[1], GROUPS)).reshape((GROUPS, GROUP_TOK)).astype(jnp.int32)
    request_of_position = jax.vmap(lambda own: jnp.searchsorted(jnp.cumsum(uneven_parts(own, REQS, GROUP_TOK, MOST_REQ, 2)), jnp.arange(GROUP_TOK), side="right"))(jax.random.split(splits[2], GROUPS)).reshape((GROUPS, GROUP_TOK)).astype(jnp.int32)
    expert_ids_keys = jax.random.split(jax.random.fold_in(splits[3], 1), GROUPS * GROUP_TOK // TOK_DEV)
    expert_ids_turns = jax.random.permutation(jax.random.fold_in(splits[3], 3), GROUPS * GROUP_TOK // TOK_DEV)
    expert_ids = jax.vmap(lambda own, number: routed_block(jax.random.fold_in(splits[3], 2), own, number, TOK_DEV, EXPERTS, TOP, CAP, 1))(expert_ids_keys, expert_ids_turns).reshape((GROUPS, GROUP_TOK, TOP))
    gate_values = jnp.clip(0.1 + 0.9 * jax.random.uniform(splits[4], (GROUPS, GROUP_TOK, TOP), jnp.float32) ** level_of(splits[4], (GROUPS, GROUP_TOK, TOP), ((0, 16), (1, 8)), -0.2, 0.2), 0.1, 1.0)
    attn_norm = jnp.clip(1.0 + 0.15 * jax.random.normal(splits[5], (D,), jnp.float32), 0.25, 1.75).astype(jnp.bfloat16)
    moe_norm = jnp.clip(1.0 + 0.15 * jax.random.normal(splits[6], (D,), jnp.float32), 0.25, 1.75).astype(jnp.bfloat16)
    w_query = gaussian(splits[7], (D, HEADS * HD), D ** -0.5, 0.125, ((1, 8),))
    w_latent = gaussian(splits[8], (D, LAT), D ** -0.5, 0.125)
    w_key_up = draw_w_key_up(jax.random.fold_in(splits[18], 71), 0)
    w_value_up = gaussian(splits[10], (LAT, HEADS * HD), LAT ** -0.5, 0.25, ((1, 8),))
    w_output = gaussian(splits[11], (HEADS * HD, D), (HEADS * HD) ** -0.5, 0.125, ((0, 8),))
    w_shared_gate = gaussian(splits[12], (D, SHARED_FF), D ** -0.5, 0.125, ((1, 8),))
    w_shared_up = gaussian(splits[13], (D, SHARED_FF), D ** -0.5, 0.125, ((1, 8),))
    w_shared_down = gaussian(splits[14], (SHARED_FF, D), SHARED_FF ** -0.5, 0.109375, ((0, 8),))
    w_routed_gate = gaussian(splits[15], (HALVES, D, FFH), D ** -0.5, 0.125, ((0, 128),))
    w_routed_up = gaussian(splits[16], (HALVES, D, FFH), D ** -0.5, 0.125, ((0, 128),))
    w_routed_down = gaussian(splits[17], (HALVES, FFH, D), FF ** -0.5, 0.15625, ((0, 128),))
    return {"tokens": tokens, "position_of_row": position_of_row, "request_of_position": request_of_position, "expert_ids": expert_ids, "gate_values": gate_values, "attn_norm": attn_norm, "moe_norm": moe_norm, "w_query": w_query, "w_latent": w_latent, "w_key_up": w_key_up, "w_value_up": w_value_up, "w_output": w_output, "w_shared_gate": w_shared_gate, "w_shared_up": w_shared_up, "w_shared_down": w_shared_down, "w_routed_gate": w_routed_gate, "w_routed_up": w_routed_up, "w_routed_down": w_routed_down}


epsilon = 1e-06
score_scale = 192.0 ** (-0.5)

def rms_scale(values, gain):
    widened = values.astype(jnp.float32)
    mean_square = lax.optimization_barrier(jnp.mean(widened * widened, axis=-1, keepdims=True))
    return (widened * lax.rsqrt(mean_square + epsilon) * gain.astype(jnp.float32)).astype(jnp.bfloat16)

def one_head(normed, latent, allowed, head_weights):
    weight_query, weight_key, weight_value = head_weights
    queries = jnp.dot(normed, weight_query, preferred_element_type=jnp.float32).astype(jnp.bfloat16)
    query_latent = jnp.dot(queries, weight_key.T, preferred_element_type=jnp.float32).astype(jnp.bfloat16)
    scores = jnp.dot(query_latent, latent.T, preferred_element_type=jnp.float32) * score_scale
    scores = jnp.where(allowed, scores, -1e+30)
    largest = lax.optimization_barrier(jnp.max(scores, axis=1, keepdims=True))
    raised = jnp.exp(scores - largest)
    probs = (raised / lax.optimization_barrier(jnp.sum(raised, axis=1, keepdims=True))).astype(jnp.bfloat16)
    mixed = jnp.dot(probs, latent, preferred_element_type=jnp.float32).astype(jnp.bfloat16)
    return jnp.dot(mixed, weight_value, preferred_element_type=jnp.float32).astype(jnp.bfloat16)

def reference(tokens, position_of_row, request_of_position, expert_ids, gate_values, attn_norm, moe_norm, w_query, w_latent, w_key_up, w_value_up, w_output, w_shared_gate, w_shared_up, w_shared_down, w_routed_gate, w_routed_up, w_routed_down):
    head_query = w_query.reshape(D, HEADS, HD).transpose(1, 0, 2)
    head_key = w_key_up.reshape(LAT, HEADS, HD).transpose(1, 0, 2)
    head_value = w_value_up.reshape(LAT, HEADS, HD).transpose(1, 0, 2)

    def group_layer(group_inputs):
        group_rows, positions, requests_table = group_inputs
        requests = jnp.take(requests_table, positions)
        allowed = (requests[:, None] == requests[None, :]) & (positions[None, :] <= positions[:, None])
        normed = rms_scale(group_rows, attn_norm)
        latent = jnp.dot(normed, w_latent, preferred_element_type=jnp.float32).astype(jnp.bfloat16)
        heads_out = lax.map(lambda weights: one_head(normed, latent, allowed, weights), (head_query, head_key, head_value))
        joined = heads_out.transpose(1, 0, 2).reshape(GROUP_TOK, HEADS * HD)
        attended = jnp.dot(joined, w_output, preferred_element_type=jnp.float32)
        return (group_rows.astype(jnp.float32) + attended).astype(jnp.bfloat16)
    resid = lax.map(group_layer, (tokens, position_of_row, request_of_position))
    resid_flat = resid.reshape(GROUPS * GROUP_TOK, D)
    moe_in = rms_scale(resid_flat, moe_norm)
    shared_gate = jnp.dot(moe_in, w_shared_gate, preferred_element_type=jnp.float32)
    shared_up = jnp.dot(moe_in, w_shared_up, preferred_element_type=jnp.float32)
    shared_hidden = (jax.nn.silu(shared_gate) * shared_up).astype(jnp.bfloat16)
    shared_out = jnp.dot(shared_hidden, w_shared_down, preferred_element_type=jnp.float32)
    flat_ids = expert_ids.reshape(-1)
    flat_gate = gate_values.reshape(-1)
    slots_all = DEVICES * CAP
    gate_stack = w_routed_gate.reshape(EXPERTS, 2, D, FFH)
    up_stack = w_routed_up.reshape(EXPERTS, 2, D, FFH)
    down_stack = w_routed_down.reshape(EXPERTS, 2, FFH, D)

    def expert_step(carry, step_inputs):
        expert, gate_weight, up_weight, down_weight = step_inputs
        hits = flat_ids == expert
        found = jnp.sum(hits.astype(jnp.int32))
        entries = jnp.nonzero(hits, size=slots_all, fill_value=0)[0].astype(jnp.int32)
        valid = jnp.arange(slots_all, dtype=jnp.int32) < found
        token_rows = (entries // TOP).astype(jnp.int32)
        chosen = jnp.take(moe_in, token_rows, axis=0)
        outputs = []
        for which_half in range(2):
            gate_proj = jnp.dot(chosen, gate_weight[which_half], preferred_element_type=jnp.float32)
            up_proj = jnp.dot(chosen, up_weight[which_half], preferred_element_type=jnp.float32)
            activated = (jax.nn.silu(gate_proj) * up_proj).astype(jnp.bfloat16)
            outputs.append(jnp.dot(activated, down_weight[which_half], preferred_element_type=jnp.float32).astype(jnp.bfloat16))
        expert_out = (outputs[0].astype(jnp.float32) + outputs[1].astype(jnp.float32)).astype(jnp.bfloat16)
        weighting = jnp.where(valid, jnp.take(flat_gate, entries), jnp.zeros_like(flat_gate[:1]))
        carry = carry.at[token_rows].add(expert_out.astype(jnp.float32) * weighting[:, None])
        return (carry, None)
    routed_out, unused = lax.scan(expert_step, jnp.zeros((GROUPS * GROUP_TOK, D), jnp.float32), (jnp.arange(EXPERTS, dtype=jnp.int32), gate_stack, up_stack, down_stack))
    layer_out = (resid_flat.astype(jnp.float32) + shared_out + routed_out).astype(jnp.bfloat16)
    return layer_out.reshape(GROUPS, GROUP_TOK, D)
```

```python
import jax
import jax.numpy as jnp
from jax import lax
from jax.sharding import Mesh
from jax.sharding import PartitionSpec as P

HD = 128
LAT = 512
CAP = 16

SEQ = ("xl", "z")
EXP = ("xh", "y", "c")
ALL = SEQ + EXP

epsilon = 1e-06
score_scale = 192.0 ** (-0.5)
f32 = jnp.float32
bf16 = jnp.bfloat16


def rms_scale(values, gain):
    widened = values.astype(f32)
    mean_square = jnp.mean(widened * widened, axis=-1, keepdims=True)
    return (widened * lax.rsqrt(mean_square + epsilon) * gain.astype(f32)).astype(bf16)


def swiglu_rows(rows_in, gate_weight, up_weight):
    gate_proj = jnp.dot(rows_in, gate_weight, preferred_element_type=f32)
    up_proj = jnp.dot(rows_in, up_weight, preferred_element_type=f32)
    return (jax.nn.silu(gate_proj) * up_proj).astype(bf16)


def ring(count, step):
    return [(i, (i + step) % count) for i in range(count)]


def gather_pieces(own):
    half = own.shape[0] // 2
    up = ring(4, 1)
    down = ring(4, -1)
    flip = ring(2, 1)
    side = lax.ppermute(own, "xl", flip)
    below = lax.ppermute(own, "z", up)
    above = lax.ppermute(own, "z", down)
    far_low = lax.ppermute(below[:half], "z", up)
    far_high = lax.ppermute(above[half:], "z", down)
    side_below = lax.ppermute(side, "z", up)
    side_above = lax.ppermute(side, "z", down)
    side_far_low = lax.ppermute(far_low, "xl", flip)
    side_far_high = lax.ppermute(far_high, "xl", flip)
    return (
        (0, 0, 0, own),
        (1, 0, 0, side),
        (0, 3, 0, below),
        (0, 1, 0, above),
        (0, 2, 0, far_low),
        (0, 2, half, far_high),
        (1, 3, 0, side_below),
        (1, 1, 0, side_above),
        (1, 2, 0, side_far_low),
        (1, 2, half, side_far_high),
    )


def place_of(dx, dz):
    xl = lax.axis_index("xl")
    z = lax.axis_index("z")
    return ((xl + dx) % 2) * 4 + (z + dz) % 4


def gather_rows(own):
    rows, width = own.shape
    out = jnp.zeros((8 * rows, width), own.dtype)
    for dx, dz, start, piece in gather_pieces(own):
        out = lax.dynamic_update_slice(out, piece, (place_of(dx, dz) * rows + start, 0))
    return out


def gather_columns(own):
    rows, width = own.shape
    out = jnp.zeros((rows, 8 * width), own.dtype)
    for dx, dz, start, piece in gather_pieces(own):
        out = lax.dynamic_update_slice(out, piece, (start, place_of(dx, dz) * width))
    return out


def swap_cores(values):
    return lax.ppermute(values, "c", [(0, 1), (1, 0)])


def shards(
    tokens,
    position_of_row,
    request_of_position,
    expert_ids,
    gate_values,
    attn_norm,
    moe_norm,
    w_query,
    w_latent,
    w_key_up,
    w_value_up,
    w_output,
    w_shared_gate,
    w_shared_up,
    w_shared_down,
    w_routed_gate,
    w_routed_up,
    w_routed_down,
):
    own = tokens[0]
    rows, width = own.shape
    heads_here = w_query.shape[1] // HD
    here = place_of(0, 0)
    core = lax.axis_index("c")
    experts = 64

    tokens_all = gather_rows(own)

    part = w_output.shape[0] // 2
    mine = lax.dynamic_slice(w_output, (core * part, 0), (part, width))
    gathered = lax.all_gather(mine, SEQ, axis=0, tiled=False)
    swapped = swap_cores(gathered)
    w_out = jnp.where(
        core == 0,
        jnp.concatenate([gathered, swapped], axis=1),
        jnp.concatenate([swapped, gathered], axis=1),
    ).reshape(-1, width)

    other_gate = swap_cores(w_routed_gate[0])
    other_up = swap_cores(w_routed_up[0])
    other_down = swap_cores(w_routed_down[0])

    ids = expert_ids[0]
    named = ids[:, :, None] == jnp.arange(experts, dtype=jnp.int32)[None, None, :]
    chosen = jnp.any(named, axis=1)
    gate_of = jnp.sum(jnp.where(named, gate_values[0][:, :, None], 0.0), axis=1)
    order = jnp.arange(rows)
    before = (order[None, :] < order[:, None]).astype(bf16)
    earlier = jnp.dot(before, chosen.astype(bf16), preferred_element_type=f32)
    slot = jnp.where(chosen, earlier, -1.0).astype(jnp.int32)
    hit = slot[:, :, None] == jnp.arange(CAP, dtype=jnp.int32)[None, None, :]
    hit = hit.reshape(rows, experts * CAP)
    weights = jnp.repeat(gate_of, CAP, axis=1)
    weights = jnp.where(hit, weights, 0.0)
    high = lax.reduce_precision(weights, 8, 7)
    rest = weights - high
    middle = lax.reduce_precision(rest, 8, 7)
    low = rest - middle
    mixing = jnp.concatenate([high, middle, low], axis=0).astype(bf16)
    spread = hit.astype(bf16)

    normed = rms_scale(tokens_all, attn_norm)
    latent = jnp.dot(normed, w_latent, preferred_element_type=f32).astype(bf16)
    queries = jnp.dot(normed, w_query, preferred_element_type=f32).astype(bf16)
    positions = position_of_row[0]
    requests = jnp.take(request_of_position[0], positions)
    allowed = (requests[:, None] == requests[None, :]) & (positions[None, :] <= positions[:, None])
    joined = []
    for head in range(heads_here):
        cols = slice(head * HD, (head + 1) * HD)
        query_latent = lax.dot_general(
            queries[:, cols], w_key_up[:, cols], (((1,), (1,)), ((), ())), preferred_element_type=f32
        ).astype(bf16)
        scores = jnp.dot(query_latent, latent.T, preferred_element_type=f32) * score_scale
        scores = jnp.where(allowed, scores, -1e30)
        largest = jnp.max(scores, axis=1, keepdims=True)
        raised = jnp.exp(scores - largest)
        probs = (raised / jnp.sum(raised, axis=1, keepdims=True)).astype(bf16)
        mixed = jnp.dot(probs, latent, preferred_element_type=f32).astype(bf16)
        head_out = jnp.dot(mixed, w_value_up[:, cols], preferred_element_type=f32).astype(bf16)
        joined.append(gather_columns(head_out))
    w_out = w_out.reshape(8, heads_here, HD, width)

    def attend(pick):
        total = 0.0
        for head in range(heads_here):
            total = total + jnp.dot(
                pick(joined[head]),
                w_out[:, head].reshape(-1, width),
                preferred_element_type=f32,
            )
        return total

    def pick_own(v):
        return lax.dynamic_slice(v, (here * rows, 0), (rows, v.shape[1]))

    resid = (own.astype(f32) + attend(pick_own)).astype(bf16)
    moe_own = rms_scale(resid, moe_norm)

    outgoing = lax.dot_general(
        spread, moe_own, (((0,), (0,)), ((), ())), preferred_element_type=f32
    ).astype(bf16)
    slots = outgoing.shape[0]
    arrived = lax.all_to_all(
        outgoing.reshape(128, slots // 128, width), ALL, split_axis=0, concat_axis=0, tiled=True
    ).reshape(slots, width)

    resid_all = (tokens_all.astype(f32) + attend(lambda v: v)).astype(bf16)
    moe_all = rms_scale(resid_all, moe_norm)
    shared_hidden = swiglu_rows(moe_all, w_shared_gate, w_shared_up)
    shared_out = lax.psum_scatter(
        jnp.dot(shared_hidden, w_shared_down, preferred_element_type=f32).astype(bf16),
        SEQ,
        scatter_dimension=0,
        tiled=True,
    ).astype(f32)

    halves = []
    for gate_w, up_w, down_w in (
        (w_routed_gate[0], w_routed_up[0], w_routed_down[0]),
        (other_gate, other_up, other_down),
    ):
        hidden = swiglu_rows(arrived, gate_w, up_w)
        halves.append(jnp.dot(hidden, down_w, preferred_element_type=f32).astype(bf16))
    expert_out = (halves[0].astype(f32) + halves[1].astype(f32)).astype(bf16)
    returned = lax.all_to_all(
        expert_out.reshape(128, slots // 128, width), ALL, split_axis=0, concat_axis=0, tiled=True
    ).reshape(slots, width)
    parts = jnp.dot(mixing, returned, preferred_element_type=f32).reshape(3, rows, width)
    routed_out = parts[0] + parts[1] + parts[2]
    layer_out = (resid.astype(f32) + shared_out + routed_out).astype(bf16)
    return layer_out.reshape(1, rows, width)


def solution(mesh):
    fine = Mesh(mesh.devices.reshape(2, 4, 2, 4, 2), ALL)
    in_specs = (
        P(EXP, SEQ, None),
        P(EXP, None),
        P(EXP, None),
        P(EXP, SEQ, None),
        P(EXP, SEQ, None),
        P(),
        P(),
        P(None, SEQ),
        P(),
        P(None, SEQ),
        P(None, SEQ),
        P(SEQ, None),
        P(None, SEQ),
        P(None, SEQ),
        P(SEQ, None),
        P(ALL, None, None),
        P(ALL, None, None),
        P(ALL, None, None),
    )
    out_specs = P(EXP, SEQ, None)
    return jax.shard_map(shards, mesh=fine, in_specs=in_specs, out_specs=out_specs, check_vma=False)
```

```python
import jax
import jax.numpy as jnp
from jax import lax
from jax.experimental import pallas as pl
from jax.experimental.pallas import tpu as pltpu
from jax.sharding import Mesh
from jax.sharding import PartitionSpec as P

HD = 128
LAT = 512
CAP = 16

SEQ = ("xl", "z")
EXP = ("xh", "y", "c")
ALL = SEQ + EXP

epsilon = 1e-06
exponent_scale = 192.0 ** (-0.5) * 1.4426950408889634
f32 = jnp.float32
bf16 = jnp.bfloat16


def rms_scale(values, gain):
    widened = values.astype(f32)
    mean_square = jnp.mean(widened * widened, axis=-1, keepdims=True)
    return (widened * lax.rsqrt(mean_square + epsilon) * gain.astype(f32)).astype(bf16)


def swiglu_rows(rows_in, gate_weight, up_weight):
    gate_proj = jnp.dot(rows_in, gate_weight, preferred_element_type=f32)
    up_proj = jnp.dot(rows_in, up_weight, preferred_element_type=f32)
    return (jax.nn.silu(gate_proj) * up_proj).astype(bf16)


def ring(count, step):
    return [(i, (i + step) % count) for i in range(count)]


def gather_pieces(own, beside_first=None, beside_second=None):
    half = own.shape[0] // 2
    up = ring(4, 1)
    down = ring(4, -1)
    flip = ring(2, 1)
    below = lax.ppermute(own, "z", up)
    above = lax.ppermute(own, "z", down)
    side = lax.ppermute(own, "xl", flip)
    (below, above, side), beside_first = together((below, above, side), beside_first)
    far_low = lax.ppermute(below[:half], "z", up)
    far_high = lax.ppermute(above[half:], "z", down)
    side_below = lax.ppermute(side, "z", up)
    side_above = lax.ppermute(side, "z", down)
    (far_low, far_high), beside_second = together((far_low, far_high), beside_second)
    side_far_low = lax.ppermute(far_low, "xl", flip)
    side_far_high = lax.ppermute(far_high, "xl", flip)
    pieces = (
        (0, 0, 0, own),
        (0, 3, 0, below),
        (0, 1, 0, above),
        (1, 0, 0, side),
        (0, 2, 0, far_low),
        (0, 2, half, far_high),
        (1, 3, 0, side_below),
        (1, 1, 0, side_above),
        (1, 2, 0, side_far_low),
        (1, 2, half, side_far_high),
    )
    return pieces, beside_first, beside_second


def together(values, others):
    if others is None:
        return values, None
    return lax.optimization_barrier((values, others))


def place_of(dx, dz):
    xl = lax.axis_index("xl")
    z = lax.axis_index("z")
    return ((xl + dx) % 2) * 4 + (z + dz) % 4


def gather_rows(own, beside_first, beside_second):
    rows, width = own.shape
    out = jnp.zeros((8 * rows, width), own.dtype)
    pieces, beside_first, beside_second = gather_pieces(own, beside_first, beside_second)
    for dx, dz, start, piece in pieces:
        out = lax.dynamic_update_slice(out, piece, (place_of(dx, dz) * rows + start, 0))
    return out, beside_first, beside_second


def gather_columns(own):
    rows, width = own.shape
    out = jnp.zeros((rows, 8 * width), own.dtype)
    for dx, dz, start, piece in gather_pieces(own)[0]:
        out = lax.dynamic_update_slice(out, piece, (start, place_of(dx, dz) * width))
    return out


def swap_cores(values):
    return lax.ppermute(values, "c", [(0, 1), (1, 0)])


def attention(tokens_all, gain, w_latent, w_query, w_key_up, w_value_up, marks_row, marks_col, block=512):
    rows, width = tokens_all.shape
    heads = w_query.shape[1] // HD
    blocks = rows // block

    def body(x_ref, gain_ref, wl_ref, wq_ref, wk_ref, wv_ref, mr_ref, mc_ref, out_ref, lat_ref, ql_ref):
        phase = pl.program_id(0)
        start = pl.multiple_of(pl.program_id(1) * block, block)

        @pl.when(phase == 0)
        def _():
            x = x_ref[...].astype(f32)
            mean_square = jnp.mean(x * x, axis=-1, keepdims=True)
            normed = (x * lax.rsqrt(mean_square + epsilon) * gain_ref[...].astype(f32)).astype(bf16)
            lat = jnp.dot(normed, wl_ref[...], preferred_element_type=f32)
            lat_ref[pl.ds(start, block), :] = lat.astype(bf16)
            queries = jnp.dot(normed, wq_ref[...], preferred_element_type=f32).astype(bf16)
            for head in range(heads):
                cols = slice(head * HD, (head + 1) * HD)
                ql = lax.dot_general(
                    queries[:, cols], wk_ref[:, cols], (((1,), (1,)), ((), ())), preferred_element_type=f32
                )
                ql_ref[head, pl.ds(start, block), :] = ql.astype(bf16)

        @pl.when(phase == 1)
        def _():
            lat = lat_ref[...]
            seen = (mc_ref[0:1, :] <= mr_ref[:, 0:1]) & (mc_ref[1:2, :] == mr_ref[:, 1:2])
            for head in range(heads):
                cols = slice(head * HD, (head + 1) * HD)
                ql = ql_ref[head, pl.ds(start, block), :]
                scores = lax.dot_general(
                    ql, lat, (((1,), (1,)), ((), ())), preferred_element_type=f32
                )
                scores = jnp.where(seen, scores, -1e30)
                largest = jnp.max(scores, axis=1, keepdims=True)
                raised = jnp.exp2((scores - largest) * exponent_scale)
                total = jnp.sum(raised, axis=1, keepdims=True)
                mixed = jnp.dot(raised.astype(bf16), lat, preferred_element_type=f32)
                mixed = (mixed * (1.0 / total)).astype(bf16)
                out_ref[:, cols] = jnp.dot(
                    mixed, wv_ref[:, cols], preferred_element_type=f32
                ).astype(bf16)

    whole = lambda a: pl.BlockSpec(a.shape, lambda p, i: (0,) * a.ndim)
    return pl.pallas_call(
        body,
        grid=(2, blocks),
        in_specs=[
            pl.BlockSpec((block, width), lambda p, i: (jnp.where(p == 0, i, blocks - 1), 0)),
            whole(gain),
            whole(w_latent),
            whole(w_query),
            whole(w_key_up),
            whole(w_value_up),
            pl.BlockSpec((block, 2), lambda p, i: (jnp.where(p == 0, 0, i), 0)),
            whole(marks_col),
        ],
        out_specs=pl.BlockSpec((block, heads * HD), lambda p, i: (jnp.where(p == 0, 0, i), 0)),
        out_shape=jax.ShapeDtypeStruct((rows, heads * HD), bf16),
        scratch_shapes=[pltpu.VMEM((rows, LAT), bf16), pltpu.VMEM((heads, rows, LAT), bf16)],
        compiler_params=pltpu.CompilerParams(
            dimension_semantics=("arbitrary", "arbitrary"), vmem_limit_bytes=58 * 1024 * 1024
        ),
        name="attend",
    )(tokens_all, gain, w_latent, w_query, w_key_up, w_value_up, marks_row, marks_col)


def run_shared(joined, tokens_all, w_out, gain, w_gate, w_up, w_down, block=256):
    rows, width = tokens_all.shape

    def body(j_ref, x_ref, wo_ref, gain_ref, wg_ref, wu_ref, wd_ref, out_ref):
        attended = jnp.dot(j_ref[...], wo_ref[...], preferred_element_type=f32)
        resid = (x_ref[...].astype(f32) + attended).astype(bf16).astype(f32)
        mean_square = jnp.mean(resid * resid, axis=-1, keepdims=True)
        moe_in = (resid * lax.rsqrt(mean_square + epsilon) * gain_ref[...].astype(f32)).astype(bf16)
        across = (((1,), (1,)), ((), ()))
        gate = lax.dot_general(moe_in, wg_ref[...], across, preferred_element_type=f32)
        up = lax.dot_general(moe_in, wu_ref[...], across, preferred_element_type=f32)
        act = (gate * (1.0 / (1.0 + jnp.exp(-gate))) * up).astype(bf16)
        out_ref[...] = jnp.dot(act, wd_ref[...], preferred_element_type=f32).astype(bf16)

    whole = lambda a: pl.BlockSpec(a.shape, lambda i: (0,) * a.ndim)
    by_rows = lambda a: pl.BlockSpec((block, a.shape[1]), lambda i: (i, 0))
    operands = (joined, tokens_all, w_out, gain, w_gate, w_up, w_down)
    return pl.pallas_call(
        body,
        grid=(rows // block,),
        in_specs=[by_rows(joined), by_rows(tokens_all)] + [whole(a) for a in operands[2:]],
        out_specs=by_rows(tokens_all),
        out_shape=jax.ShapeDtypeStruct((rows, width), bf16),
        compiler_params=pltpu.CompilerParams(
            dimension_semantics=("arbitrary",), vmem_limit_bytes=58 * 1024 * 1024
        ),
        cost_estimate=pl.CostEstimate(flops=1, bytes_accessed=1, transcendentals=0),
        name="shared",
    )(*operands)


def run_experts(x, weights, block=512):
    rows, width = x.shape
    hidden = weights[0].shape[0]
    blocks = rows // block

    def body(x_ref, g0, u0, d0, g1, u1, d1, out_ref, gs, us, ds, sems):
        copies = []
        for half, (g, u, d) in enumerate(((g0, u0, d0), (g1, u1, d1))):
            copies.append(
                (
                    pltpu.make_async_copy(g, gs.at[half], sems.at[half, 0]),
                    pltpu.make_async_copy(u, us.at[half], sems.at[half, 1]),
                    pltpu.make_async_copy(d, ds.at[half], sems.at[half, 2]),
                )
            )
        for trio in copies:
            for one in trio:
                one.start()
        for half in range(2):
            for one in copies[half]:
                one.wait()

            def step(i, carry):
                at = pl.ds(pl.multiple_of(i * block, block), block)
                xb = x_ref[at, :]
                gate = lax.dot_general(xb, gs[half], (((1,), (1,)), ((), ())), preferred_element_type=f32)
                up = lax.dot_general(xb, us[half], (((1,), (1,)), ((), ())), preferred_element_type=f32)
                act = (gate * (1.0 / (1.0 + jnp.exp(-gate))) * up).astype(bf16)
                res = jnp.dot(act, ds[half], preferred_element_type=f32).astype(bf16)
                if half == 0:
                    out_ref[at, :] = res
                else:
                    out_ref[at, :] = (out_ref[at, :].astype(f32) + res.astype(f32)).astype(bf16)
                return carry

            lax.fori_loop(0, blocks, step, 0, unroll=True)

    hbm = pl.BlockSpec(memory_space=pl.ANY)
    vm = pl.BlockSpec(memory_space=pltpu.VMEM)
    return pl.pallas_call(
        body,
        in_specs=[vm] + [hbm] * 6,
        out_specs=vm,
        out_shape=jax.ShapeDtypeStruct((rows, width), bf16),
        scratch_shapes=[
            pltpu.VMEM((2, hidden, width), bf16),
            pltpu.VMEM((2, hidden, width), bf16),
            pltpu.VMEM((2, hidden, width), bf16),
            pltpu.SemaphoreType.DMA((2, 3)),
        ],
        compiler_params=pltpu.CompilerParams(vmem_limit_bytes=60 * 1024 * 1024),
        name="experts",
    )(x, *weights)


def shards(
    tokens,
    position_of_row,
    request_of_position,
    expert_ids,
    gate_values,
    attn_norm,
    moe_norm,
    w_query,
    w_latent,
    w_key_up,
    w_value_up,
    w_output,
    w_shared_gate,
    w_shared_up,
    w_shared_down,
    w_routed_gate,
    w_routed_up,
    w_routed_down,
):
    own = tokens[0]
    rows, width = own.shape
    here = place_of(0, 0)
    core = lax.axis_index("c")
    experts = 64

    positions = position_of_row[0]
    requests = jnp.take(request_of_position[0], positions)
    marks = jnp.stack([positions, requests], axis=1), jnp.stack([positions, requests], axis=0)

    ids = expert_ids[0]
    named = ids[:, :, None] == jnp.arange(experts, dtype=jnp.int32)[None, None, :]
    chosen = jnp.any(named, axis=1)
    gate_of = jnp.sum(jnp.where(named, gate_values[0][:, :, None], 0.0), axis=1)
    order = jnp.arange(rows)
    before = (order[None, :] < order[:, None]).astype(bf16)
    earlier = jnp.dot(before, chosen.astype(bf16), preferred_element_type=f32)
    slot = jnp.where(chosen, earlier, -1.0).astype(jnp.int32)
    hit = slot[:, :, None] == jnp.arange(CAP, dtype=jnp.int32)[None, None, :]
    hit = hit.reshape(rows, experts * CAP)
    weights = jnp.repeat(gate_of, CAP, axis=1)
    weights = jnp.where(hit, weights, 0.0)
    high = lax.reduce_precision(weights, 8, 7)
    rest = weights - high
    middle = lax.reduce_precision(rest, 8, 7)
    low = rest - middle
    mixing = jnp.concatenate([high, middle, low], axis=0).astype(bf16)
    spread = hit.astype(bf16)

    tokens_all, marks, _ = gather_rows(own, marks, None)

    part = w_output.shape[0] // 2
    mine = lax.dynamic_slice(w_output, (core * part, 0), (part, width))
    own_half = (w_routed_gate[0].T, w_routed_up[0].T, w_routed_down[0])
    mine, own_half, tokens_all = lax.optimization_barrier((mine, own_half, tokens_all))
    other_half = tuple(swap_cores(w) for w in own_half)
    w_out = lax.all_gather(mine, SEQ + ("c",), axis=0, tiled=True)

    head_out = attention(
        tokens_all,
        attn_norm.reshape(1, -1),
        w_latent,
        w_query,
        w_key_up,
        w_value_up,
        *marks,
    )
    head_out, other_half = lax.optimization_barrier((head_out, other_half))
    joined = gather_columns(head_out)

    joined_own = lax.dynamic_slice(joined, (here * rows, 0), (rows, joined.shape[1]))
    attended = jnp.dot(joined_own, w_out, preferred_element_type=f32)
    resid = (own.astype(f32) + attended).astype(bf16)
    moe_own = rms_scale(resid, moe_norm)

    outgoing = lax.dot_general(
        spread, moe_own, (((0,), (0,)), ((), ())), preferred_element_type=f32
    ).astype(bf16)
    outgoing, joined = lax.optimization_barrier((outgoing, joined))
    slots = outgoing.shape[0]
    arrived = lax.all_to_all(
        outgoing.reshape(128, slots // 128, width), ALL, split_axis=0, concat_axis=0, tiled=True
    ).reshape(slots, width)

    shared_part = run_shared(
        joined,
        tokens_all,
        w_out,
        moe_norm.reshape(1, -1),
        w_shared_gate.T,
        w_shared_up.T,
        w_shared_down,
    )
    shared_out = lax.psum_scatter(
        shared_part,
        SEQ,
        scatter_dimension=0,
        tiled=True,
    ).astype(f32)

    expert_out = run_experts(arrived, own_half + other_half)
    returned = lax.all_to_all(
        expert_out.reshape(128, slots // 128, width), ALL, split_axis=0, concat_axis=0, tiled=True
    ).reshape(slots, width)
    parts = jnp.dot(mixing, returned, preferred_element_type=f32).reshape(3, rows, width)
    routed_out = parts[0] + parts[1] + parts[2]
    layer_out = (resid.astype(f32) + shared_out + routed_out).astype(bf16)
    return layer_out.reshape(1, rows, width)


def solution(mesh):
    fine = Mesh(mesh.devices.reshape(2, 4, 2, 4, 2), ALL)
    in_specs = (
        P(EXP, SEQ, None),
        P(EXP, None),
        P(EXP, None),
        P(EXP, SEQ, None),
        P(EXP, SEQ, None),
        P(),
        P(),
        P(None, SEQ),
        P(),
        P(None, SEQ),
        P(None, SEQ),
        P(SEQ, None),
        P(None, SEQ),
        P(None, SEQ),
        P(SEQ, None),
        P(ALL, None, None),
        P(ALL, None, None),
        P(ALL, None, None),
    )
    out_specs = P(EXP, SEQ, None)
    return jax.shard_map(shards, mesh=fine, in_specs=in_specs, out_specs=out_specs, check_vma=False)
```

```python
import jax
import jax.numpy as jnp
from jax import lax
from jax.experimental import pallas as pl
from jax.experimental.pallas import tpu as pltpu
from jax.sharding import Mesh
from jax.sharding import PartitionSpec as P

HD = 128
LAT = 512
CAP = 16

SEQ = ("xl", "z")
EXP = ("xh", "y", "c")
ALL = SEQ + EXP

epsilon = 1e-06
exponent_scale = 192.0 ** (-0.5) * 1.4426950408889634
f32 = jnp.float32
bf16 = jnp.bfloat16


def ring(count, step):
    return [(i, (i + step) % count) for i in range(count)]


def gather_pieces(own, beside=None):
    half = own.shape[0] // 2
    up = ring(4, 1)
    down = ring(4, -1)
    flip = ring(2, 1)
    below = lax.ppermute(own, "z", up)
    above = lax.ppermute(own, "z", down)
    side = lax.ppermute(own, "xl", flip)
    (below, above, side), beside = together((below, above, side), beside)
    side_below = lax.ppermute(below, "xl", flip)
    side_above = lax.ppermute(side, "z", down)
    far = lax.ppermute(below, "z", up)
    side_far_low = lax.ppermute(side_below[:half], "z", up)
    side_far_high = lax.ppermute(side_above[half:], "z", down)
    pieces = (
        (0, 0, 0, own),
        (0, 3, 0, below),
        (0, 1, 0, above),
        (1, 0, 0, side),
        (1, 3, 0, side_below),
        (1, 1, 0, side_above),
        (0, 2, 0, far),
        (1, 2, 0, side_far_low),
        (1, 2, half, side_far_high),
    )
    return pieces, beside


def together(values, others):
    if others is None:
        return values, None
    return lax.optimization_barrier((values, others))


def place_of(dx, dz):
    xl = lax.axis_index("xl")
    z = lax.axis_index("z")
    return ((xl + dx) % 2) * 4 + (z + dz) % 4


def gather_rows(own, beside):
    rows, width = own.shape
    out = jnp.zeros((8 * rows, width), own.dtype)
    pieces, beside = gather_pieces(own, beside)
    for dx, dz, start, piece in pieces:
        out = lax.dynamic_update_slice(out, piece, (place_of(dx, dz) * rows + start, 0))
    return out, beside


def gather_columns(own):
    rows, width = own.shape
    out = jnp.zeros((rows, 8 * width), own.dtype)
    for dx, dz, start, piece in gather_pieces(own)[0]:
        out = lax.dynamic_update_slice(out, piece, (start, place_of(dx, dz) * width))
    return out


def swap_cores(values):
    return lax.ppermute(values, "c", [(0, 1), (1, 0)])


def attention(tokens_all, gain, w_latent, w_query, w_key_up, w_value_up, marks_row, marks_col, block=512):
    rows, width = tokens_all.shape
    heads = w_query.shape[1] // HD
    blocks = rows // block

    def body(x_ref, gain_ref, wl_ref, wq_ref, wk_ref, wv_ref, mr_ref, mc_ref, out_ref, lat_ref, ql_ref):
        phase = pl.program_id(0)
        start = pl.multiple_of(pl.program_id(1) * block, block)

        @pl.when(phase == 0)
        def _():
            x = x_ref[...].astype(f32)
            mean_square = jnp.mean(x * x, axis=-1, keepdims=True)
            normed = (x * lax.rsqrt(mean_square + epsilon) * gain_ref[...].astype(f32)).astype(bf16)
            lat = jnp.dot(normed, wl_ref[...], preferred_element_type=f32)
            lat_ref[pl.ds(start, block), :] = lat.astype(bf16)
            queries = jnp.dot(normed, wq_ref[...], preferred_element_type=f32).astype(bf16)
            for head in range(heads):
                cols = slice(head * HD, (head + 1) * HD)
                ql = lax.dot_general(
                    queries[:, cols], wk_ref[:, cols], (((1,), (1,)), ((), ())), preferred_element_type=f32
                )
                ql_ref[head, pl.ds(start, block), :] = ql.astype(bf16)

        @pl.when(phase == 1)
        def _():
            lat = lat_ref[...]
            seen = (mc_ref[0:1, :] <= mr_ref[:, 0:1]) & (mc_ref[1:2, :] == mr_ref[:, 1:2])
            for head in range(heads):
                cols = slice(head * HD, (head + 1) * HD)
                ql = ql_ref[head, pl.ds(start, block), :]
                scores = lax.dot_general(
                    ql, lat, (((1,), (1,)), ((), ())), preferred_element_type=f32
                )
                scores = jnp.where(seen, scores, -1e30)
                largest = jnp.max(scores, axis=1, keepdims=True)
                raised = jnp.exp2((scores - largest) * exponent_scale)
                total = jnp.sum(raised, axis=1, keepdims=True)
                mixed = jnp.dot(raised.astype(bf16), lat, preferred_element_type=f32)
                mixed = (mixed * (1.0 / total)).astype(bf16)
                out_ref[:, cols] = jnp.dot(
                    mixed, wv_ref[:, cols], preferred_element_type=f32
                ).astype(bf16)

    whole = lambda a: pl.BlockSpec(a.shape, lambda p, i: (0,) * a.ndim)
    return pl.pallas_call(
        body,
        grid=(2, blocks),
        in_specs=[
            pl.BlockSpec((block, width), lambda p, i: (jnp.where(p == 0, i, blocks - 1), 0)),
            whole(gain),
            whole(w_latent),
            whole(w_query),
            whole(w_key_up),
            whole(w_value_up),
            pl.BlockSpec((block, 2), lambda p, i: (jnp.where(p == 0, 0, i), 0)),
            whole(marks_col),
        ],
        out_specs=pl.BlockSpec((block, heads * HD), lambda p, i: (jnp.where(p == 0, 0, i), 0)),
        out_shape=jax.ShapeDtypeStruct((rows, heads * HD), bf16),
        scratch_shapes=[pltpu.VMEM((rows, LAT), bf16), pltpu.VMEM((heads, rows, LAT), bf16)],
        compiler_params=pltpu.CompilerParams(
            dimension_semantics=("arbitrary", "arbitrary"), vmem_limit_bytes=58 * 1024 * 1024
        ),
        name="attend",
    )(tokens_all, gain, w_latent, w_query, w_key_up, w_value_up, marks_row, marks_col)


def run_dispatch(here, joined, own, w_out, gain, spread, together_of=2, slot_block=256):
    rows, width = own.shape
    pieces, inner, span = w_out.shape
    slots = spread.shape[0]
    first = pieces // together_of
    last = slots // slot_block

    def body(here_ref, j_ref, x_ref, wo_ref, gain_ref, spread_ref, resid_ref, out_ref, moe_ref):
        step = pl.program_id(0)
        for now in range(first):

            @pl.when(step == now)
            def _():
                for part in range(together_of):
                    start = (now * together_of + part) * span
                    cols = slice(start, start + span)
                    attended = jnp.dot(j_ref[...], wo_ref[part], preferred_element_type=f32)
                    added = x_ref[:, cols].astype(f32) + attended
                    resid_ref[:, cols] = added.astype(bf16)

        @pl.when(step == first)
        def _():
            resid = resid_ref[...].astype(f32)
            mean_square = jnp.mean(resid * resid, axis=-1, keepdims=True)
            normed = resid * lax.rsqrt(mean_square + epsilon) * gain_ref[...].astype(f32)
            moe_ref[...] = normed.astype(bf16)

        @pl.when(step >= first)
        def _():
            out_ref[...] = jnp.dot(
                spread_ref[...], moe_ref[...], preferred_element_type=f32
            ).astype(bf16)

    late = lambda i: jnp.maximum(i - first, 0)
    return pl.pallas_call(
        body,
        grid_spec=pltpu.PrefetchScalarGridSpec(
            num_scalar_prefetch=1,
            grid=(first + last,),
            in_specs=[
                pl.BlockSpec((rows, inner), lambda i, h: (h[0], 0)),
                pl.BlockSpec((rows, width), lambda i, h: (0, 0)),
                pl.BlockSpec(
                    (together_of, inner, span), lambda i, h: (jnp.minimum(i, first - 1), 0, 0)
                ),
                pl.BlockSpec((1, width), lambda i, h: (0, 0)),
                pl.BlockSpec((slot_block, rows), lambda i, h: (late(i), 0)),
            ],
            out_specs=[
                pl.BlockSpec((rows, width), lambda i, h: (0, 0)),
                pl.BlockSpec((slot_block, width), lambda i, h: (late(i), 0)),
            ],
            scratch_shapes=[pltpu.VMEM((rows, width), bf16)],
        ),
        out_shape=[
            jax.ShapeDtypeStruct((rows, width), bf16),
            jax.ShapeDtypeStruct((slots, width), bf16),
        ],
        compiler_params=pltpu.CompilerParams(
            dimension_semantics=("arbitrary",), vmem_limit_bytes=58 * 1024 * 1024
        ),
        name="dispatch",
    )(here.reshape(1), joined, own, w_out, gain, spread)


def run_combine(mixing, returned, resid, shared_out, block=512):
    rows, width = resid.shape

    def body(m_ref, r_ref, resid_ref, shared_ref, out_ref):
        parts = jnp.dot(m_ref[...], r_ref[...], preferred_element_type=f32)
        routed = parts[:rows] + parts[rows : 2 * rows] + parts[2 * rows :]
        total = resid_ref[...].astype(f32) + shared_ref[...].astype(f32) + routed
        out_ref[...] = total.astype(bf16)

    by_cols = lambda a: pl.BlockSpec((a.shape[0], block), lambda i: (0, i))
    return pl.pallas_call(
        body,
        grid=(width // block,),
        in_specs=[
            pl.BlockSpec(mixing.shape, lambda i: (0, 0)),
            by_cols(returned),
            by_cols(resid),
            by_cols(shared_out),
        ],
        out_specs=by_cols(resid),
        out_shape=jax.ShapeDtypeStruct((rows, width), bf16),
        compiler_params=pltpu.CompilerParams(
            dimension_semantics=("arbitrary",), vmem_limit_bytes=58 * 1024 * 1024
        ),
        name="combine",
    )(mixing, returned, resid, shared_out)


def run_shared(joined, tokens_all, w_out, gain, w_gate, w_up, w_down, block=256):
    rows, width = tokens_all.shape
    pieces, _, span = w_out.shape

    def body(j_ref, x_ref, wo_ref, gain_ref, wg_ref, wu_ref, wd_ref, out_ref, res_ref):
        for piece in range(pieces):
            cols = slice(piece * span, (piece + 1) * span)
            attended = jnp.dot(j_ref[...], wo_ref[piece], preferred_element_type=f32)
            added = x_ref[:, cols].astype(f32) + attended
            res_ref[:, cols] = added.astype(bf16)
        resid = res_ref[...].astype(f32)
        mean_square = jnp.mean(resid * resid, axis=-1, keepdims=True)
        moe_in = (resid * lax.rsqrt(mean_square + epsilon) * gain_ref[...].astype(f32)).astype(bf16)
        across = (((1,), (1,)), ((), ()))
        gate = lax.dot_general(moe_in, wg_ref[...], across, preferred_element_type=f32)
        up = lax.dot_general(moe_in, wu_ref[...], across, preferred_element_type=f32)
        act = (gate * (1.0 / (1.0 + jnp.exp(-gate))) * up).astype(bf16)
        out_ref[...] = jnp.dot(act, wd_ref[...], preferred_element_type=f32).astype(bf16)

    whole = lambda a: pl.BlockSpec(a.shape, lambda i: (0,) * a.ndim)
    by_rows = lambda a: pl.BlockSpec((block, a.shape[1]), lambda i: (i, 0))
    operands = (joined, tokens_all, w_out, gain, w_gate, w_up, w_down)
    return pl.pallas_call(
        body,
        grid=(rows // block,),
        in_specs=[by_rows(joined), by_rows(tokens_all)] + [whole(a) for a in operands[2:]],
        out_specs=by_rows(tokens_all),
        out_shape=jax.ShapeDtypeStruct((rows, width), bf16),
        scratch_shapes=[pltpu.VMEM((block, width), bf16)],
        compiler_params=pltpu.CompilerParams(
            dimension_semantics=("arbitrary",), vmem_limit_bytes=58 * 1024 * 1024
        ),
        cost_estimate=pl.CostEstimate(
            flops=13_000_000_000, bytes_accessed=25_000_000, transcendentals=720_000
        ),
        name="shared",
    )(*operands)


def run_experts(x, weights, block=512):
    rows, width = x.shape
    hidden = weights[0].shape[0]
    blocks = rows // block

    def body(x_ref, g0, u0, d0, g1, u1, d1, out_ref, gs, us, ds, sems):
        copies = []
        for half, (g, u, d) in enumerate(((g0, u0, d0), (g1, u1, d1))):
            copies.append(
                (
                    pltpu.make_async_copy(g, gs.at[half], sems.at[half, 0]),
                    pltpu.make_async_copy(u, us.at[half], sems.at[half, 1]),
                    pltpu.make_async_copy(d, ds.at[half], sems.at[half, 2]),
                )
            )
        for trio in copies:
            for one in trio:
                one.start()
        for half in range(2):
            for one in copies[half]:
                one.wait()

            def step(i, carry):
                at = pl.ds(pl.multiple_of(i * block, block), block)
                xb = x_ref[at, :]
                gate = lax.dot_general(xb, gs[half], (((1,), (1,)), ((), ())), preferred_element_type=f32)
                up = lax.dot_general(xb, us[half], (((1,), (1,)), ((), ())), preferred_element_type=f32)
                act = (gate * (1.0 / (1.0 + jnp.exp(-gate))) * up).astype(bf16)
                res = jnp.dot(act, ds[half], preferred_element_type=f32).astype(bf16)
                if half == 0:
                    out_ref[at, :] = res
                else:
                    out_ref[at, :] = (out_ref[at, :].astype(f32) + res.astype(f32)).astype(bf16)
                return carry

            lax.fori_loop(0, blocks, step, 0, unroll=True)

    hbm = pl.BlockSpec(memory_space=pl.ANY)
    vm = pl.BlockSpec(memory_space=pltpu.VMEM)
    return pl.pallas_call(
        body,
        in_specs=[vm] + [hbm] * 6,
        out_specs=vm,
        out_shape=jax.ShapeDtypeStruct((rows, width), bf16),
        scratch_shapes=[
            pltpu.VMEM((2, hidden, width), bf16),
            pltpu.VMEM((2, hidden, width), bf16),
            pltpu.VMEM((2, hidden, width), bf16),
            pltpu.SemaphoreType.DMA((2, 3)),
        ],
        compiler_params=pltpu.CompilerParams(vmem_limit_bytes=60 * 1024 * 1024),
        name="experts",
    )(x, *weights)


def shards(
    tokens,
    position_of_row,
    request_of_position,
    expert_ids,
    gate_values,
    attn_norm,
    moe_norm,
    w_query,
    w_latent,
    w_key_up,
    w_value_up,
    w_output,
    w_shared_gate,
    w_shared_up,
    w_shared_down,
    w_routed_gate,
    w_routed_up,
    w_routed_down,
):
    own = tokens[0]
    rows, width = own.shape
    here = place_of(0, 0)
    core = lax.axis_index("c")
    experts = 64

    positions = position_of_row[0]
    requests = jnp.take(request_of_position[0], positions)
    marks = jnp.stack([positions, requests], axis=1), jnp.stack([positions, requests], axis=0)

    ids = expert_ids[0]
    named = ids[:, :, None] == jnp.arange(experts, dtype=jnp.int32)[None, None, :]
    chosen = jnp.any(named, axis=1)
    gate_of = jnp.sum(jnp.where(named, gate_values[0][:, :, None], 0.0), axis=1)
    order = jnp.arange(rows)
    before = (order[None, :] < order[:, None]).astype(bf16)
    earlier = jnp.dot(before, chosen.astype(bf16), preferred_element_type=f32)
    slot = jnp.where(chosen, earlier, -1.0).astype(jnp.int32)
    hit = slot[:, :, None] == jnp.arange(CAP, dtype=jnp.int32)[None, None, :]
    hit = hit.reshape(rows, experts * CAP)
    weights = jnp.repeat(gate_of, CAP, axis=1)
    weights = jnp.where(hit, weights, 0.0)
    high = lax.reduce_precision(weights, 8, 7)
    rest = weights - high
    middle = lax.reduce_precision(rest, 8, 7)
    low = rest - middle
    mixing = jnp.concatenate([high, middle, low], axis=0).astype(bf16)
    spread = hit.astype(bf16).T

    span = w_output.shape[1] // 8
    block_here = lax.axis_index("y") * 2 + core
    columns = lax.dynamic_slice(w_output, (0, block_here * span), (w_output.shape[0], span))
    columns = lax.all_gather(columns, SEQ, axis=0, tiled=True)

    tokens_all, marks = gather_rows(own, marks)

    own_half = (w_routed_gate[0].T, w_routed_up[0].T, w_routed_down[0])
    columns, own_half, tokens_all = lax.optimization_barrier((columns, own_half, tokens_all))
    other_half = tuple(swap_cores(w) for w in own_half)
    w_out = lax.all_gather(columns, ("y", "c"), axis=0, tiled=False)

    head_out = attention(
        tokens_all,
        attn_norm.reshape(1, -1),
        w_latent,
        w_query,
        w_key_up,
        w_value_up,
        *marks,
    )
    head_out, other_half = lax.optimization_barrier((head_out, other_half))
    joined = gather_columns(head_out)

    resid, outgoing = run_dispatch(here, joined, own, w_out, moe_norm.reshape(1, -1), spread)
    outgoing, joined = lax.optimization_barrier((outgoing, joined))
    slots = outgoing.shape[0]
    arrived = lax.all_to_all(
        outgoing.reshape(128, slots // 128, width), ALL, split_axis=0, concat_axis=0, tiled=True
    ).reshape(slots, width)

    shared_part = run_shared(
        joined,
        tokens_all,
        w_out,
        moe_norm.reshape(1, -1),
        w_shared_gate.T,
        w_shared_up.T,
        w_shared_down,
    )
    arrived, shared_part = lax.optimization_barrier((arrived, shared_part))
    shared_out = lax.psum_scatter(
        shared_part,
        SEQ,
        scatter_dimension=0,
        tiled=True,
    )

    expert_out = run_experts(arrived, own_half + other_half)
    returned = lax.all_to_all(
        expert_out.reshape(128, slots // 128, width), ALL, split_axis=0, concat_axis=0, tiled=True
    ).reshape(slots, width)
    layer_out = run_combine(mixing, returned, resid, shared_out)
    return layer_out.reshape(1, rows, width)


def solution(mesh):
    fine = Mesh(mesh.devices.reshape(2, 4, 2, 4, 2), ALL)
    in_specs = (
        P(EXP, SEQ, None),
        P(EXP, None),
        P(EXP, None),
        P(EXP, SEQ, None),
        P(EXP, SEQ, None),
        P(),
        P(),
        P(None, SEQ),
        P(),
        P(None, SEQ),
        P(None, SEQ),
        P(SEQ, None),
        P(None, SEQ),
        P(None, SEQ),
        P(SEQ, None),
        P(ALL, None, None),
        P(ALL, None, None),
        P(ALL, None, None),
    )
    out_specs = P(EXP, SEQ, None)
    return jax.shard_map(shards, mesh=fine, in_specs=in_specs, out_specs=out_specs, check_vma=False)
```

```python
import jax
import jax.numpy as jnp
from jax import lax
from jax.experimental import pallas as pl
from jax.experimental.pallas import tpu as pltpu
from jax.sharding import Mesh
from jax.sharding import PartitionSpec as P

HD = 128
LAT = 512
CAP = 16

SEQ = ("xl", "z")
EXP = ("xh", "y", "c")
ALL = SEQ + EXP

epsilon = 1e-06
exponent_scale = 192.0 ** (-0.5) * 1.4426950408889634
f32 = jnp.float32
bf16 = jnp.bfloat16


def ring(count, step):
    return [(i, (i + step) % count) for i in range(count)]


def gather_pieces(own):
    half = own.shape[0] // 2
    up = ring(4, 1)
    down = ring(4, -1)
    flip = ring(2, 1)
    below = lax.ppermute(own, "z", up)
    above = lax.ppermute(own, "z", down)
    side = lax.ppermute(own, "xl", flip)
    far = lax.ppermute(below, "z", up)
    side_below = lax.ppermute(below, "xl", flip)
    side_above = lax.ppermute(side, "z", down)
    side_far_low = lax.ppermute(side_below[:half], "z", up)
    side_far_high = lax.ppermute(side_above[half:], "z", down)
    pieces = (
        (0, 0, 0, own),
        (0, 3, 0, below),
        (0, 1, 0, above),
        (1, 0, 0, side),
        (1, 3, 0, side_below),
        (1, 1, 0, side_above),
        (0, 2, 0, far),
        (1, 2, 0, side_far_low),
        (1, 2, half, side_far_high),
    )
    return pieces


def place_of(dx, dz):
    xl = lax.axis_index("xl")
    z = lax.axis_index("z")
    return ((xl + dx) % 2) * 4 + (z + dz) % 4


def gather_rows(own):
    rows, width = own.shape
    out = set_down(own, place_of(0, 0))
    for dx, dz, start, piece in gather_pieces(own)[1:]:
        out = lax.dynamic_update_slice(out, piece, (place_of(dx, dz) * rows + start, 0))
    return out


def set_down(own, place):
    def body(place_ref, own_ref, out_ref):
        out_ref[...] = own_ref[...]

    return pl.pallas_call(
        body,
        grid_spec=pltpu.PrefetchScalarGridSpec(
            num_scalar_prefetch=1,
            grid=(1,),
            in_specs=[pl.BlockSpec(own.shape, lambda i, p: (0, 0))],
            out_specs=pl.BlockSpec(own.shape, lambda i, p: (p[0], 0)),
        ),
        out_shape=jax.ShapeDtypeStruct((8 * own.shape[0], own.shape[1]), own.dtype),
        name="set_down",
    )(place.reshape(1), own)


def gather_columns(own, out):
    rows, width = own.shape
    for dx, dz, start, piece in gather_pieces(own)[1:]:
        out = lax.dynamic_update_slice(out, piece, (start, place_of(dx, dz) * width))
    return out


def swap_cores(values):
    return lax.ppermute(values, "c", [(0, 1), (1, 0)])


def attention(tokens_all, gain, w_latent, w_query, w_key_up, w_value_up, positions, request_table, here, block=512):
    rows, width = tokens_all.shape
    heads = w_query.shape[1] // HD
    blocks = rows // block

    def body(
        here_ref,
        x_ref,
        gain_ref,
        wl_ref,
        wq_ref,
        wk_ref,
        wv_ref,
        pos_ref,
        table_ref,
        out_ref,
        all_ref,
        lat_ref,
        ql_ref,
        marks_ref,
    ):
        phase = pl.program_id(0)
        start = pl.multiple_of(pl.program_id(1) * block, block)

        @pl.when((phase == 0) & (start == 0))
        def _():
            position = pos_ref[...].astype(f32)
            table = table_ref[...].astype(f32)
            request = jnp.zeros_like(position)
            for value in range(1, 4):
                first = jnp.sum((table < value).astype(f32), axis=1, keepdims=True)
                request = request + (position >= first).astype(f32)
            marks_ref[0:1, :] = position
            marks_ref[1:2, :] = request
            marks_ref[2:8, :] = jnp.zeros((6, rows), f32)

        @pl.when(phase == 0)
        def _():
            x = x_ref[...].astype(f32)
            mean_square = jnp.mean(x * x, axis=-1, keepdims=True)
            normed = (x * lax.rsqrt(mean_square + epsilon) * gain_ref[...].astype(f32)).astype(bf16)
            lat = jnp.dot(normed, wl_ref[...], preferred_element_type=f32)
            lat_ref[pl.ds(start, block), :] = lat.astype(bf16)
            queries = jnp.dot(normed, wq_ref[...], preferred_element_type=f32).astype(bf16)
            for head in range(heads):
                cols = slice(head * HD, (head + 1) * HD)
                ql = lax.dot_general(
                    queries[:, cols], wk_ref[:, cols], (((1,), (1,)), ((), ())), preferred_element_type=f32
                )
                ql_ref[head, pl.ds(start, block), :] = ql.astype(bf16)

        @pl.when(phase == 1)
        def _():
            lat = lat_ref[...]
            down = marks_ref[:, pl.ds(start, block)].T
            seen = (marks_ref[0:1, :] <= down[:, 0:1]) & (marks_ref[1:2, :] == down[:, 1:2])
            for head in range(heads):
                cols = slice(head * HD, (head + 1) * HD)
                ql = ql_ref[head, pl.ds(start, block), :]
                scores = lax.dot_general(
                    ql, lat, (((1,), (1,)), ((), ())), preferred_element_type=f32
                )
                scores = jnp.where(seen, scores, -1e30)
                largest = jnp.max(scores, axis=1, keepdims=True)
                raised = jnp.exp2((scores - largest) * exponent_scale)
                total = jnp.sum(raised, axis=1, keepdims=True)
                mixed = jnp.dot(raised.astype(bf16), lat, preferred_element_type=f32)
                mixed = (mixed * (1.0 / total)).astype(bf16)
                head_out = jnp.dot(mixed, wv_ref[:, cols], preferred_element_type=f32).astype(bf16)
                out_ref[:, cols] = head_out
                all_ref[:, cols] = head_out

    whole = lambda a: pl.BlockSpec(a.shape, lambda p, i, h: (0,) * a.ndim)
    late = lambda p, i: jnp.where(p == 0, 0, i)
    return pl.pallas_call(
        body,
        grid_spec=pltpu.PrefetchScalarGridSpec(
            num_scalar_prefetch=1,
            grid=(2, blocks),
            in_specs=[
                pl.BlockSpec((block, width), lambda p, i, h: (jnp.where(p == 0, i, blocks - 1), 0)),
                whole(gain),
                whole(w_latent),
                whole(w_query),
                whole(w_key_up),
                whole(w_value_up),
                whole(positions),
                whole(request_table),
            ],
            out_specs=[
                pl.BlockSpec((block, heads * HD), lambda p, i, h: (late(p, i), 0)),
                pl.BlockSpec((block, heads * HD), lambda p, i, h: (late(p, i), h[0])),
            ],
            scratch_shapes=[
                pltpu.VMEM((rows, LAT), bf16),
                pltpu.VMEM((heads, rows, LAT), bf16),
                pltpu.VMEM((8, rows), f32),
            ],
        ),
        out_shape=[
            jax.ShapeDtypeStruct((rows, heads * HD), bf16),
            jax.ShapeDtypeStruct((rows, 8 * heads * HD), bf16),
        ],
        compiler_params=pltpu.CompilerParams(
            dimension_semantics=("arbitrary", "arbitrary"), vmem_limit_bytes=58 * 1024 * 1024
        ),
        name="attend",
    )(
        here.reshape(1),
        tokens_all,
        gain,
        w_latent,
        w_query,
        w_key_up,
        w_value_up,
        positions,
        request_table,
    )


def run_dispatch(here, joined, own, w_out, gain, spread, together_of=2, slot_block=256):
    rows, width = own.shape
    pieces, inner, span = w_out.shape
    slots = spread.shape[0]
    first = pieces // together_of
    last = slots // slot_block

    def body(here_ref, j_ref, x_ref, wo_ref, gain_ref, spread_ref, resid_ref, out_ref, moe_ref):
        step = pl.program_id(0)

        @pl.when(step < first)
        def _():
            for part in range(together_of):
                start = (step * together_of + part) * span
                cols = pl.ds(pl.multiple_of(start, span), span)
                attended = jnp.dot(j_ref[...], wo_ref[part], preferred_element_type=f32)
                added = x_ref[:, cols].astype(f32) + attended
                resid_ref[:, cols] = added.astype(bf16)

        @pl.when(step == first)
        def _():
            resid = resid_ref[...].astype(f32)
            mean_square = jnp.mean(resid * resid, axis=-1, keepdims=True)
            normed = resid * lax.rsqrt(mean_square + epsilon) * gain_ref[...].astype(f32)
            moe_ref[...] = normed.astype(bf16)

        @pl.when(step >= first)
        def _():
            out_ref[...] = jnp.dot(
                spread_ref[...], moe_ref[...], preferred_element_type=f32
            ).astype(bf16)

    late = lambda i: jnp.maximum(i - first, 0)
    return pl.pallas_call(
        body,
        grid_spec=pltpu.PrefetchScalarGridSpec(
            num_scalar_prefetch=1,
            grid=(first + last,),
            in_specs=[
                pl.BlockSpec((rows, inner), lambda i, h: (h[0], 0)),
                pl.BlockSpec((rows, width), lambda i, h: (0, 0)),
                pl.BlockSpec(
                    (together_of, inner, span), lambda i, h: (jnp.minimum(i, first - 1), 0, 0)
                ),
                pl.BlockSpec((1, width), lambda i, h: (0, 0)),
                pl.BlockSpec((slot_block, rows), lambda i, h: (late(i), 0)),
            ],
            out_specs=[
                pl.BlockSpec((rows, width), lambda i, h: (0, 0)),
                pl.BlockSpec((slot_block, width), lambda i, h: (late(i), 0)),
            ],
            scratch_shapes=[pltpu.VMEM((rows, width), bf16)],
        ),
        out_shape=[
            jax.ShapeDtypeStruct((rows, width), bf16),
            jax.ShapeDtypeStruct((slots, width), bf16),
        ],
        compiler_params=pltpu.CompilerParams(
            dimension_semantics=("arbitrary",), vmem_limit_bytes=58 * 1024 * 1024
        ),
        name="dispatch",
    )(here.reshape(1), joined, own, w_out, gain, spread)


def run_combine(mixing, returned, resid, shared_out, block=512):
    rows, width = resid.shape

    def body(m_ref, r_ref, resid_ref, shared_ref, out_ref):
        parts = jnp.dot(m_ref[...], r_ref[...], preferred_element_type=f32)
        routed = parts[:rows] + parts[rows : 2 * rows] + parts[2 * rows :]
        total = resid_ref[...].astype(f32) + shared_ref[...].astype(f32) + routed
        out_ref[...] = total.astype(bf16)

    by_cols = lambda a: pl.BlockSpec((a.shape[0], block), lambda i: (0, i))
    return pl.pallas_call(
        body,
        grid=(width // block,),
        in_specs=[
            pl.BlockSpec(mixing.shape, lambda i: (0, 0)),
            by_cols(returned),
            by_cols(resid),
            by_cols(shared_out),
        ],
        out_specs=by_cols(resid),
        out_shape=jax.ShapeDtypeStruct((rows, width), bf16),
        compiler_params=pltpu.CompilerParams(
            dimension_semantics=("arbitrary",), vmem_limit_bytes=58 * 1024 * 1024
        ),
        name="combine",
    )(mixing, returned, resid, shared_out)


def run_shared(joined, tokens_all, w_out, gain, w_gate, w_up, w_down, block=256):
    rows, width = tokens_all.shape
    pieces, _, span = w_out.shape

    def body(j_ref, x_ref, wo_ref, gain_ref, wg_ref, wu_ref, wd_ref, out_ref, res_ref):
        for piece in range(pieces):
            cols = slice(piece * span, (piece + 1) * span)
            attended = jnp.dot(j_ref[...], wo_ref[piece], preferred_element_type=f32)
            added = x_ref[:, cols].astype(f32) + attended
            res_ref[:, cols] = added.astype(bf16)
        resid = res_ref[...].astype(f32)
        mean_square = jnp.mean(resid * resid, axis=-1, keepdims=True)
        moe_in = (resid * lax.rsqrt(mean_square + epsilon) * gain_ref[...].astype(f32)).astype(bf16)
        across = (((1,), (1,)), ((), ()))
        gate = lax.dot_general(moe_in, wg_ref[...], across, preferred_element_type=f32)
        up = lax.dot_general(moe_in, wu_ref[...], across, preferred_element_type=f32)
        act = (gate * (1.0 / (1.0 + jnp.exp(-gate))) * up).astype(bf16)
        out_ref[...] = jnp.dot(act, wd_ref[...], preferred_element_type=f32).astype(bf16)

    whole = lambda a: pl.BlockSpec(a.shape, lambda i: (0,) * a.ndim)
    by_rows = lambda a: pl.BlockSpec((block, a.shape[1]), lambda i: (i, 0))
    operands = (joined, tokens_all, w_out, gain, w_gate, w_up, w_down)
    return pl.pallas_call(
        body,
        grid=(rows // block,),
        in_specs=[by_rows(joined), by_rows(tokens_all)] + [whole(a) for a in operands[2:]],
        out_specs=by_rows(tokens_all),
        out_shape=jax.ShapeDtypeStruct((rows, width), bf16),
        scratch_shapes=[pltpu.VMEM((block, width), bf16)],
        compiler_params=pltpu.CompilerParams(
            dimension_semantics=("arbitrary",), vmem_limit_bytes=58 * 1024 * 1024
        ),
        cost_estimate=pl.CostEstimate(
            flops=13_000_000_000, bytes_accessed=25_000_000, transcendentals=720_000
        ),
        name="shared",
    )(*operands)


def run_experts(x, weights, block=512):
    rows, width = x.shape
    hidden = weights[0].shape[0]
    blocks = rows // block

    def body(x_ref, g0, u0, d0, g1, u1, d1, out_ref, gs, us, ds, sems):
        copies = []
        for half, (g, u, d) in enumerate(((g0, u0, d0), (g1, u1, d1))):
            copies.append(
                (
                    pltpu.make_async_copy(g, gs.at[half], sems.at[half, 0]),
                    pltpu.make_async_copy(u, us.at[half], sems.at[half, 1]),
                    pltpu.make_async_copy(d, ds.at[half], sems.at[half, 2]),
                )
            )
        for trio in copies:
            for one in trio:
                one.start()
        for half in range(2):
            for one in copies[half]:
                one.wait()

            def step(i, carry):
                at = pl.ds(pl.multiple_of(i * block, block), block)
                xb = x_ref[at, :]
                gate = lax.dot_general(xb, gs[half], (((1,), (1,)), ((), ())), preferred_element_type=f32)
                up = lax.dot_general(xb, us[half], (((1,), (1,)), ((), ())), preferred_element_type=f32)
                act = (gate * (1.0 / (1.0 + jnp.exp(-gate))) * up).astype(bf16)
                res = jnp.dot(act, ds[half], preferred_element_type=f32).astype(bf16)
                if half == 0:
                    out_ref[at, :] = res
                else:
                    out_ref[at, :] = (out_ref[at, :].astype(f32) + res.astype(f32)).astype(bf16)
                return carry

            lax.fori_loop(0, blocks, step, 0)

    hbm = pl.BlockSpec(memory_space=pl.ANY)
    vm = pl.BlockSpec(memory_space=pltpu.VMEM)
    return pl.pallas_call(
        body,
        in_specs=[vm] + [hbm] * 6,
        out_specs=vm,
        out_shape=jax.ShapeDtypeStruct((rows, width), bf16),
        scratch_shapes=[
            pltpu.VMEM((2, hidden, width), bf16),
            pltpu.VMEM((2, hidden, width), bf16),
            pltpu.VMEM((2, hidden, width), bf16),
            pltpu.SemaphoreType.DMA((2, 3)),
        ],
        compiler_params=pltpu.CompilerParams(vmem_limit_bytes=60 * 1024 * 1024),
        cost_estimate=pl.CostEstimate(
            flops=17_700_000_000, bytes_accessed=30_000_000, transcendentals=1_500_000
        ),
        name="experts",
    )(x, *weights)


def routing_tables(ids, gates, experts=64):
    top, rows = ids.shape
    slots = experts * CAP

    def body(ids_ref, gates_ref, spread_ref, mixing_ref):
        expert = lax.broadcasted_iota(jnp.int32, (experts, rows), 0)
        chosen = jnp.zeros((experts, rows), f32)
        gate_of = jnp.zeros((experts, rows), f32)
        for route in range(top):
            named = ids_ref[route : route + 1, :] == expert
            chosen = jnp.where(named, 1.0, chosen)
            gate_of = jnp.where(named, gates_ref[route : route + 1, :], gate_of)
        line = lax.broadcasted_iota(jnp.int32, (rows, rows), 0)
        before = (line < lax.broadcasted_iota(jnp.int32, (rows, rows), 1)).astype(f32).astype(bf16)
        earlier = jnp.dot(chosen.astype(bf16), before, preferred_element_type=f32)
        slot = jnp.where(chosen > 0.0, earlier, -1.0)

        owner = lax.broadcasted_iota(jnp.int32, (slots, experts), 0) // CAP
        owned = owner == lax.broadcasted_iota(jnp.int32, (slots, experts), 1)
        repeat = owned.astype(f32).astype(bf16)
        number = (lax.broadcasted_iota(jnp.int32, (slots, rows), 0) % CAP).astype(f32)
        tall = jnp.dot(repeat, slot.astype(bf16), preferred_element_type=f32)
        spread_ref[...] = (tall == number).astype(f32).astype(bf16)

        owner = lax.broadcasted_iota(jnp.int32, (experts, slots), 1) // CAP
        owned = owner == lax.broadcasted_iota(jnp.int32, (experts, slots), 0)
        repeat = owned.astype(f32).astype(bf16)
        number = (lax.broadcasted_iota(jnp.int32, (rows, slots), 1) % CAP).astype(f32)
        wide = jnp.dot(slot.T.astype(bf16), repeat, preferred_element_type=f32)
        hit = wide == number
        rest = gate_of.T
        for part in range(3):
            now = rest.astype(bf16)
            rest = rest - now.astype(f32)
            weights = jnp.dot(now, repeat, preferred_element_type=f32)
            mixing_ref[part * rows : (part + 1) * rows, :] = jnp.where(hit, weights, 0.0).astype(bf16)

    return pl.pallas_call(
        body,
        out_shape=[
            jax.ShapeDtypeStruct((slots, rows), bf16),
            jax.ShapeDtypeStruct((3 * rows, slots), bf16),
        ],
        name="routing",
    )(ids, gates)


def shards(
    tokens,
    position_of_row,
    request_of_position,
    expert_ids,
    gate_values,
    attn_norm,
    moe_norm,
    w_query,
    w_latent,
    w_key_up,
    w_value_up,
    w_output,
    w_shared_gate,
    w_shared_up,
    w_shared_down,
    w_routed_gate,
    w_routed_up,
    w_routed_down,
):
    own = tokens[0]
    rows, width = own.shape
    here = place_of(0, 0)
    core = lax.axis_index("c")

    spread, mixing = routing_tables(expert_ids[0].T, gate_values[0].T)

    span = w_output.shape[1] // 8
    block_here = lax.axis_index("y") * 2 + core
    columns = lax.dynamic_slice(w_output, (0, block_here * span), (w_output.shape[0], span))
    columns = lax.all_gather(columns, SEQ, axis=0, tiled=True)

    tokens_all = gather_rows(own)

    own_half = (w_routed_gate[0].T, w_routed_up[0].T, w_routed_down[0])
    columns, own_half, tokens_all = lax.optimization_barrier((columns, own_half, tokens_all))
    other_half = tuple(swap_cores(w) for w in own_half)
    w_out = lax.all_gather(columns, ("y", "c"), axis=0, tiled=False)

    head_out, joined = attention(
        tokens_all,
        attn_norm.reshape(1, -1),
        w_latent,
        w_query,
        w_key_up,
        w_value_up,
        position_of_row,
        request_of_position,
        here,
    )
    head_out, other_half = lax.optimization_barrier((head_out, other_half))
    joined = gather_columns(head_out, joined)

    resid, outgoing = run_dispatch(here, joined, own, w_out, moe_norm.reshape(1, -1), spread)
    outgoing, joined = lax.optimization_barrier((outgoing, joined))
    slots = outgoing.shape[0]
    arrived = lax.all_to_all(
        outgoing.reshape(128, slots // 128, width), ALL, split_axis=0, concat_axis=0, tiled=True
    ).reshape(slots, width)

    shared_part = run_shared(
        joined,
        tokens_all,
        w_out,
        moe_norm.reshape(1, -1),
        w_shared_gate.T,
        w_shared_up.T,
        w_shared_down,
    )
    arrived, _ = lax.optimization_barrier((arrived, shared_part))
    shared_out = lax.psum_scatter(
        shared_part,
        SEQ,
        scatter_dimension=0,
        tiled=True,
    )

    expert_out = run_experts(arrived, own_half + other_half)
    returned = lax.all_to_all(
        expert_out.reshape(128, slots // 128, width), ALL, split_axis=0, concat_axis=0, tiled=True
    ).reshape(slots, width)
    layer_out = run_combine(mixing, returned, resid, shared_out)
    return layer_out.reshape(1, rows, width)


def solution(mesh):
    fine = Mesh(mesh.devices.reshape(2, 4, 2, 4, 2), ALL)
    in_specs = (
        P(EXP, SEQ, None),
        P(EXP, None),
        P(EXP, None),
        P(EXP, SEQ, None),
        P(EXP, SEQ, None),
        P(),
        P(),
        P(None, SEQ),
        P(),
        P(None, SEQ),
        P(None, SEQ),
        P(SEQ, None),
        P(None, SEQ),
        P(None, SEQ),
        P(SEQ, None),
        P(ALL, None, None),
        P(ALL, None, None),
        P(ALL, None, None),
    )
    out_specs = P(EXP, SEQ, None)
    return jax.shard_map(shards, mesh=fine, in_specs=in_specs, out_specs=out_specs, check_vma=False)
```

```python
import jax
import jax.numpy as jnp
from jax import lax
from jax.experimental import pallas as pl
from jax.experimental.pallas import tpu as pltpu
from jax.sharding import Mesh
from jax.sharding import PartitionSpec as P

HD = 128
LAT = 512
CAP = 16

SEQ = ("xl", "z")
EXP = ("xh", "y", "c")
ALL = SEQ + EXP

epsilon = 1e-06
exponent_scale = 192.0 ** (-0.5) * 1.4426950408889634
f32 = jnp.float32
bf16 = jnp.bfloat16


def ring(count, step):
    return [(i, (i + step) % count) for i in range(count)]


def gather_pieces(own, early=None):
    half = own.shape[0] // 2
    up = ring(4, 1)
    down = ring(4, -1)
    flip = ring(2, 1)
    below = lax.ppermute(own, "z", up)
    above = lax.ppermute(own, "z", down)
    side = lax.ppermute(own, "xl", flip)
    if early is not None:
        side, early = lax.optimization_barrier((side, early))
    far = lax.ppermute(below, "z", up)
    side_below = lax.ppermute(below, "xl", flip)
    side_above = lax.ppermute(side, "z", down)
    side_far_low = lax.ppermute(side_below[:half], "z", up)
    side_far_high = lax.ppermute(side_above[half:], "z", down)
    pieces = (
        (0, 0, 0, own),
        (0, 3, 0, below),
        (0, 1, 0, above),
        (1, 0, 0, side),
        (1, 3, 0, side_below),
        (1, 1, 0, side_above),
        (0, 2, 0, far),
        (1, 2, 0, side_far_low),
        (1, 2, half, side_far_high),
    )
    return pieces, early


def place_of(dx, dz):
    xl = lax.axis_index("xl")
    z = lax.axis_index("z")
    return ((xl + dx) % 2) * 4 + (z + dz) % 4


def gather_rows(own, early):
    rows, width = own.shape
    out = set_down(own, place_of(0, 0), 0)
    pieces, early = gather_pieces(own, early)
    for dx, dz, start, piece in pieces[1:]:
        out = lax.dynamic_update_slice(out, piece, (place_of(dx, dz) * rows + start, 0))
    return out, early


def set_down(own, place, axis):
    def body(place_ref, own_ref, out_ref):
        out_ref[...] = own_ref[...]

    shape = list(own.shape)
    shape[axis] *= 8
    index = (lambda i, p: (p[0], 0)) if axis == 0 else (lambda i, p: (0, p[0]))
    return pl.pallas_call(
        body,
        grid_spec=pltpu.PrefetchScalarGridSpec(
            num_scalar_prefetch=1,
            grid=(1,),
            in_specs=[pl.BlockSpec(own.shape, lambda i, p: (0, 0))],
            out_specs=pl.BlockSpec(own.shape, index),
        ),
        out_shape=jax.ShapeDtypeStruct(shape, own.dtype),
        name="set_down",
    )(place.reshape(1), own)


def gather_columns(own):
    rows, width = own.shape
    out = set_down(own, place_of(0, 0), 1)
    for dx, dz, start, piece in gather_pieces(own)[0][1:]:
        out = lax.dynamic_update_slice(out, piece, (start, place_of(dx, dz) * width))
    return out


def swap_cores(values):
    return lax.ppermute(values, "c", [(0, 1), (1, 0)])


def attention(tokens_all, gain, w_latent, w_query, w_key_up, w_value_up, positions, request_table, block=512):
    rows, width = tokens_all.shape
    heads = w_query.shape[1] // HD
    blocks = rows // block

    def body(
        x_ref,
        gain_ref,
        wl_ref,
        wq_ref,
        wk_ref,
        wv_ref,
        pos_ref,
        table_ref,
        out_ref,
        lat_ref,
        ql_ref,
        marks_ref,
    ):
        phase = pl.program_id(0)
        start = pl.multiple_of(pl.program_id(1) * block, block)

        @pl.when((phase == 0) & (start == 0))
        def _():
            position = pos_ref[...].astype(f32)
            table = table_ref[...].astype(f32)
            request = jnp.zeros_like(position)
            for value in range(1, 4):
                first = jnp.sum((table < value).astype(f32), axis=1, keepdims=True)
                request = request + (position >= first).astype(f32)
            marks_ref[0:1, :] = position
            marks_ref[1:2, :] = request
            marks_ref[2:8, :] = jnp.zeros((6, rows), f32)

        @pl.when(phase == 0)
        def _():
            x = x_ref[...].astype(f32)
            mean_square = jnp.mean(x * x, axis=-1, keepdims=True)
            normed = (x * lax.rsqrt(mean_square + epsilon) * gain_ref[...].astype(f32)).astype(bf16)
            lat = jnp.dot(normed, wl_ref[...], preferred_element_type=f32)
            lat_ref[pl.ds(start, block), :] = lat.astype(bf16)
            queries = jnp.dot(normed, wq_ref[...], preferred_element_type=f32).astype(bf16)
            for head in range(heads):
                cols = slice(head * HD, (head + 1) * HD)
                ql = lax.dot_general(
                    queries[:, cols], wk_ref[:, cols], (((1,), (1,)), ((), ())), preferred_element_type=f32
                )
                ql_ref[head, pl.ds(start, block), :] = ql.astype(bf16)

        @pl.when(phase == 1)
        def _():
            lat = lat_ref[...]
            down = marks_ref[:, pl.ds(start, block)].T
            seen = (marks_ref[0:1, :] <= down[:, 0:1]) & (marks_ref[1:2, :] == down[:, 1:2])
            for head in range(heads):
                cols = slice(head * HD, (head + 1) * HD)
                ql = ql_ref[head, pl.ds(start, block), :]
                scores = lax.dot_general(
                    ql, lat, (((1,), (1,)), ((), ())), preferred_element_type=f32
                )
                scores = jnp.where(seen, scores, -1e30)
                largest = jnp.max(scores, axis=1, keepdims=True)
                raised = jnp.exp2((scores - largest) * exponent_scale)
                total = jnp.sum(raised, axis=1, keepdims=True)
                mixed = jnp.dot(raised.astype(bf16), lat, preferred_element_type=f32)
                mixed = (mixed * (1.0 / total)).astype(bf16)
                head_out = jnp.dot(mixed, wv_ref[:, cols], preferred_element_type=f32).astype(bf16)
                out_ref[:, cols] = head_out

    whole = lambda a: pl.BlockSpec(a.shape, lambda p, i: (0,) * a.ndim)
    late = lambda p, i: jnp.where(p == 0, 0, i)
    return pl.pallas_call(
        body,
        grid_spec=pl.GridSpec(
            grid=(2, blocks),
            in_specs=[
                pl.BlockSpec((block, width), lambda p, i: (jnp.where(p == 0, i, blocks - 1), 0)),
                whole(gain),
                whole(w_latent),
                whole(w_query),
                whole(w_key_up),
                whole(w_value_up),
                whole(positions),
                whole(request_table),
            ],
            out_specs=pl.BlockSpec((block, heads * HD), lambda p, i: (late(p, i), 0)),
            scratch_shapes=[
                pltpu.VMEM((rows, LAT), bf16),
                pltpu.VMEM((heads, rows, LAT), bf16),
                pltpu.VMEM((8, rows), f32),
            ],
        ),
        out_shape=jax.ShapeDtypeStruct((rows, heads * HD), bf16),
        compiler_params=pltpu.CompilerParams(
            dimension_semantics=("arbitrary", "arbitrary"), vmem_limit_bytes=62 * 1024 * 1024
        ),
        name="attend",
    )(
        tokens_all,
        gain,
        w_latent,
        w_query,
        w_key_up,
        w_value_up,
        positions,
        request_table,
    )


def run_dispatch(here, joined, own, w_out, gain, spread, together_of=4, slot_block=512):
    rows, width = own.shape
    pieces, inner, span = w_out.shape
    slots = spread.shape[0]
    first = pieces // together_of
    last = slots // slot_block

    def body(here_ref, j_ref, x_ref, wo_ref, gain_ref, spread_ref, resid_ref, out_ref, moe_ref):
        step = pl.program_id(0)

        @pl.when(step < first)
        def _():
            for part in range(together_of):
                start = (step * together_of + part) * span
                cols = pl.ds(pl.multiple_of(start, span), span)
                attended = jnp.dot(j_ref[...], wo_ref[part], preferred_element_type=f32)
                added = x_ref[:, cols].astype(f32) + attended
                resid_ref[:, cols] = added.astype(bf16)

        @pl.when(step == first)
        def _():
            resid = resid_ref[...].astype(f32)
            mean_square = jnp.mean(resid * resid, axis=-1, keepdims=True)
            normed = resid * lax.rsqrt(mean_square + epsilon) * gain_ref[...].astype(f32)
            moe_ref[...] = normed.astype(bf16)

        @pl.when(step >= first)
        def _():
            out_ref[...] = jnp.dot(
                spread_ref[...], moe_ref[...], preferred_element_type=f32
            ).astype(bf16)

    late = lambda i: jnp.maximum(i - first, 0)
    return pl.pallas_call(
        body,
        grid_spec=pltpu.PrefetchScalarGridSpec(
            num_scalar_prefetch=1,
            grid=(first + last,),
            in_specs=[
                pl.BlockSpec((rows, inner), lambda i, h: (h[0], 0)),
                pl.BlockSpec((rows, width), lambda i, h: (0, 0)),
                pl.BlockSpec(
                    (together_of, inner, span), lambda i, h: (jnp.minimum(i, first - 1), 0, 0)
                ),
                pl.BlockSpec((1, width), lambda i, h: (0, 0)),
                pl.BlockSpec((slot_block, rows), lambda i, h: (late(i), 0)),
            ],
            out_specs=[
                pl.BlockSpec((rows, width), lambda i, h: (0, 0)),
                pl.BlockSpec((slot_block, width), lambda i, h: (late(i), 0)),
            ],
            scratch_shapes=[pltpu.VMEM((rows, width), bf16)],
        ),
        out_shape=[
            jax.ShapeDtypeStruct((rows, width), bf16),
            jax.ShapeDtypeStruct((slots, width), bf16),
        ],
        compiler_params=pltpu.CompilerParams(
            dimension_semantics=("arbitrary",), vmem_limit_bytes=58 * 1024 * 1024
        ),
        name="dispatch",
    )(here.reshape(1), joined, own, w_out, gain, spread)


def run_combine(mixing, returned, resid, shared_out, block=512):
    rows, width = resid.shape

    def body(m_ref, r_ref, resid_ref, shared_ref, out_ref):
        parts = jnp.dot(m_ref[...], r_ref[...], preferred_element_type=f32)
        routed = parts[:rows] + parts[rows : 2 * rows] + parts[2 * rows :]
        total = resid_ref[...].astype(f32) + shared_ref[...].astype(f32) + routed
        out_ref[...] = total.astype(bf16)

    by_cols = lambda a: pl.BlockSpec((a.shape[0], block), lambda i: (0, i))
    return pl.pallas_call(
        body,
        grid=(width // block,),
        in_specs=[
            pl.BlockSpec(mixing.shape, lambda i: (0, 0)),
            by_cols(returned),
            by_cols(resid),
            by_cols(shared_out),
        ],
        out_specs=by_cols(resid),
        out_shape=jax.ShapeDtypeStruct((rows, width), bf16),
        compiler_params=pltpu.CompilerParams(
            dimension_semantics=("arbitrary",), vmem_limit_bytes=58 * 1024 * 1024
        ),
        name="combine",
    )(mixing, returned, resid, shared_out)


def run_shared(joined, tokens_all, w_out, gain, w_gate, w_up, w_down, block=256):
    rows, width = tokens_all.shape
    pieces, _, span = w_out.shape

    def body(j_ref, x_ref, wo_ref, gain_ref, wg_ref, wu_ref, wd_ref, out_ref, res_ref):
        for piece in range(pieces):
            cols = slice(piece * span, (piece + 1) * span)
            attended = jnp.dot(j_ref[...], wo_ref[piece], preferred_element_type=f32)
            added = x_ref[:, cols].astype(f32) + attended
            res_ref[:, cols] = added.astype(bf16)
        resid = res_ref[...].astype(f32)
        mean_square = jnp.mean(resid * resid, axis=-1, keepdims=True)
        moe_in = (resid * lax.rsqrt(mean_square + epsilon) * gain_ref[...].astype(f32)).astype(bf16)
        across = (((1,), (1,)), ((), ()))
        gate = lax.dot_general(moe_in, wg_ref[...], across, preferred_element_type=f32)
        up = lax.dot_general(moe_in, wu_ref[...], across, preferred_element_type=f32)
        act = (gate * (1.0 / (1.0 + jnp.exp(-gate))) * up).astype(bf16)
        out_ref[...] = jnp.dot(act, wd_ref[...], preferred_element_type=f32).astype(bf16)

    whole = lambda a: pl.BlockSpec(a.shape, lambda i: (0,) * a.ndim)
    by_rows = lambda a: pl.BlockSpec((block, a.shape[1]), lambda i: (i, 0))
    operands = (joined, tokens_all, w_out, gain, w_gate, w_up, w_down)
    return pl.pallas_call(
        body,
        grid=(rows // block,),
        in_specs=[by_rows(joined), by_rows(tokens_all)] + [whole(a) for a in operands[2:]],
        out_specs=by_rows(tokens_all),
        out_shape=jax.ShapeDtypeStruct((rows, width), bf16),
        scratch_shapes=[pltpu.VMEM((block, width), bf16)],
        compiler_params=pltpu.CompilerParams(
            dimension_semantics=("arbitrary",), vmem_limit_bytes=58 * 1024 * 1024
        ),
        cost_estimate=pl.CostEstimate(
            flops=13_000_000_000, bytes_accessed=25_000_000, transcendentals=720_000
        ),
        name="shared",
    )(*operands)


def run_experts(x, weights, block=256):
    rows, width = x.shape
    hidden = weights[0].shape[0]
    blocks = rows // block

    def body(x_hbm, g0, u0, d0, g1, u1, d1, out_hbm, xs, outs, gs, us, ds, x_sems, w_sems, out_sems):
        def load_x(i):
            at = pl.ds(i * block, block)
            return pltpu.make_async_copy(x_hbm.at[at], xs.at[at], x_sems.at[i])

        def save(i):
            at = pl.ds(i * block, block)
            return pltpu.make_async_copy(outs.at[at], out_hbm.at[at], out_sems.at[i])

        loads = []
        for half, (g, u, d) in enumerate(((g0, u0, d0), (g1, u1, d1))):
            loads.append(
                (
                    pltpu.make_async_copy(g, gs.at[half], w_sems.at[half, 0]),
                    pltpu.make_async_copy(u, us.at[half], w_sems.at[half, 1]),
                    pltpu.make_async_copy(d, ds.at[half], w_sems.at[half, 2]),
                )
            )
        load_x(0).start()
        for one in loads[0]:
            one.start()
        for i in range(1, blocks):
            load_x(i).start()
        for one in loads[1]:
            one.start()
        across = (((1,), (1,)), ((), ()))
        for half in range(2):
            for i in range(blocks):
                at = pl.ds(i * block, block)
                if half == 0:
                    load_x(i).wait()
                if i == 0:
                    loads[half][0].wait()
                xb = xs[at, :]
                gate = lax.dot_general(xb, gs[half], across, preferred_element_type=f32)
                if i == 0:
                    loads[half][1].wait()
                up = lax.dot_general(xb, us[half], across, preferred_element_type=f32)
                act = (gate * (1.0 / (1.0 + jnp.exp(-gate))) * up).astype(bf16)
                if i == 0:
                    loads[half][2].wait()
                res = jnp.dot(act, ds[half], preferred_element_type=f32).astype(bf16)
                if half == 0:
                    outs[at, :] = res
                else:
                    outs[at, :] = (outs[at, :].astype(f32) + res.astype(f32)).astype(bf16)
                    save(i).start()
        for i in range(blocks):
            save(i).wait()

    hbm = pl.BlockSpec(memory_space=pl.ANY)
    return pl.pallas_call(
        body,
        in_specs=[hbm] * 7,
        out_specs=hbm,
        out_shape=jax.ShapeDtypeStruct((rows, width), bf16),
        scratch_shapes=[
            pltpu.VMEM((rows, width), bf16),
            pltpu.VMEM((rows, width), bf16),
            pltpu.VMEM((2, hidden, width), bf16),
            pltpu.VMEM((2, hidden, width), bf16),
            pltpu.VMEM((2, hidden, width), bf16),
            pltpu.SemaphoreType.DMA((blocks,)),
            pltpu.SemaphoreType.DMA((2, 3)),
            pltpu.SemaphoreType.DMA((blocks,)),
        ],
        compiler_params=pltpu.CompilerParams(vmem_limit_bytes=60 * 1024 * 1024),
        cost_estimate=pl.CostEstimate(
            flops=17_700_000_000, bytes_accessed=30_000_000, transcendentals=1_500_000
        ),
        name="experts",
    )(x, *weights)


def routing_tables(ids, gates, experts=64):
    top, rows = ids.shape
    slots = experts * CAP

    def body(ids_ref, gates_ref, spread_ref, mixing_ref):
        expert = lax.broadcasted_iota(jnp.int32, (experts, rows), 0)
        chosen = jnp.zeros((experts, rows), f32)
        gate_of = jnp.zeros((experts, rows), f32)
        for route in range(top):
            named = ids_ref[route : route + 1, :] == expert
            chosen = jnp.where(named, 1.0, chosen)
            gate_of = jnp.where(named, gates_ref[route : route + 1, :], gate_of)
        line = lax.broadcasted_iota(jnp.int32, (rows, rows), 0)
        before = (line < lax.broadcasted_iota(jnp.int32, (rows, rows), 1)).astype(f32).astype(bf16)
        earlier = jnp.dot(chosen.astype(bf16), before, preferred_element_type=f32)
        slot = jnp.where(chosen > 0.0, earlier, -1.0)

        owner = lax.broadcasted_iota(jnp.int32, (slots, experts), 0) // CAP
        owned = owner == lax.broadcasted_iota(jnp.int32, (slots, experts), 1)
        repeat = owned.astype(f32).astype(bf16)
        number = (lax.broadcasted_iota(jnp.int32, (slots, rows), 0) % CAP).astype(f32)
        tall = jnp.dot(repeat, slot.astype(bf16), preferred_element_type=f32)
        spread_ref[...] = (tall == number).astype(f32).astype(bf16)

        owner = lax.broadcasted_iota(jnp.int32, (experts, slots), 1) // CAP
        owned = owner == lax.broadcasted_iota(jnp.int32, (experts, slots), 0)
        repeat = owned.astype(f32).astype(bf16)
        number = (lax.broadcasted_iota(jnp.int32, (rows, slots), 1) % CAP).astype(f32)
        wide = jnp.dot(slot.T.astype(bf16), repeat, preferred_element_type=f32)
        hit = wide == number
        rest = gate_of.T
        for part in range(3):
            now = rest.astype(bf16)
            rest = rest - now.astype(f32)
            weights = jnp.dot(now, repeat, preferred_element_type=f32)
            mixing_ref[part * rows : (part + 1) * rows, :] = jnp.where(hit, weights, 0.0).astype(bf16)

    return pl.pallas_call(
        body,
        out_shape=[
            jax.ShapeDtypeStruct((slots, rows), bf16),
            jax.ShapeDtypeStruct((3 * rows, slots), bf16),
        ],
        name="routing",
    )(ids, gates)


def shards(
    tokens,
    position_of_row,
    request_of_position,
    expert_ids,
    gate_values,
    attn_norm,
    moe_norm,
    w_query,
    w_latent,
    w_key_up,
    w_value_up,
    w_output,
    w_shared_gate,
    w_shared_up,
    w_shared_down,
    w_routed_gate,
    w_routed_up,
    w_routed_down,
):
    own = tokens[0]
    rows, width = own.shape
    here = place_of(0, 0)
    core = lax.axis_index("c")

    spread, mixing = routing_tables(expert_ids[0].T, gate_values[0].T)

    span = w_output.shape[1] // 8
    block_here = lax.axis_index("y") * 2 + core
    columns = lax.dynamic_slice(w_output, (0, block_here * span), (w_output.shape[0], span))
    columns = lax.all_gather(columns, SEQ, axis=0, tiled=True)

    early = (spread, mixing, attn_norm.reshape(1, -1), moe_norm.reshape(1, -1))
    tokens_all, (spread, mixing, attn_gain, moe_gain) = gather_rows(own, early)

    own_half = (w_routed_gate[0].T, w_routed_up[0].T, w_routed_down[0])
    columns, own_half, tokens_all = lax.optimization_barrier((columns, own_half, tokens_all))
    other_half = tuple(swap_cores(w) for w in own_half)
    w_out = lax.all_gather(columns, ("y", "c"), axis=0, tiled=False)

    head_out = attention(
        tokens_all,
        attn_gain,
        w_latent,
        w_query,
        w_key_up,
        w_value_up,
        position_of_row,
        request_of_position,
    )
    head_out, other_half = lax.optimization_barrier((head_out, other_half))
    joined = gather_columns(head_out)

    resid, outgoing = run_dispatch(here, joined, own, w_out, moe_gain, spread)
    outgoing, joined = lax.optimization_barrier((outgoing, joined))
    slots = outgoing.shape[0]
    arrived = lax.all_to_all(
        outgoing.reshape(128, slots // 128, width), ALL, split_axis=0, concat_axis=0, tiled=True
    ).reshape(slots, width)

    shared_part = run_shared(
        joined,
        tokens_all,
        w_out,
        moe_gain,
        w_shared_gate.T,
        w_shared_up.T,
        w_shared_down,
    )
    arrived, _ = lax.optimization_barrier((arrived, shared_part))
    shared_out = lax.psum_scatter(
        shared_part,
        SEQ,
        scatter_dimension=0,
        tiled=True,
    )

    expert_out = run_experts(arrived, own_half + other_half)
    returned = lax.all_to_all(
        expert_out.reshape(128, slots // 128, width), ALL, split_axis=0, concat_axis=0, tiled=True
    ).reshape(slots, width)
    layer_out = run_combine(mixing, returned, resid, shared_out)
    return layer_out.reshape(1, rows, width)


def solution(mesh):
    fine = Mesh(mesh.devices.reshape(2, 4, 2, 4, 2), ALL)
    in_specs = (
        P(EXP, SEQ, None),
        P(EXP, None),
        P(EXP, None),
        P(EXP, SEQ, None),
        P(EXP, SEQ, None),
        P(),
        P(),
        P(None, SEQ),
        P(),
        P(None, SEQ),
        P(None, SEQ),
        P(SEQ, None),
        P(None, SEQ),
        P(None, SEQ),
        P(SEQ, None),
        P(ALL, None, None),
        P(ALL, None, None),
        P(ALL, None, None),
    )
    out_specs = P(EXP, SEQ, None)
    return jax.shard_map(shards, mesh=fine, in_specs=in_specs, out_specs=out_specs, check_vma=False)
```

```python
import jax
import jax.numpy as jnp
from jax import lax
from jax.experimental import pallas as pl
from jax.experimental.pallas import tpu as pltpu
from jax.sharding import Mesh
from jax.sharding import PartitionSpec as P

HD = 128
LAT = 512
CAP = 16

SEQ = ("xl", "z")
EXP = ("xh", "y", "c")
ALL = SEQ + EXP

epsilon = 1e-06
exponent_scale = 192.0 ** (-0.5) * 1.4426950408889634
f32 = jnp.float32
bf16 = jnp.bfloat16


def ring(count, step):
    return [(i, (i + step) % count) for i in range(count)]


def gather_pieces(own, early=None):
    half = own.shape[0] // 2
    up = ring(4, 1)
    down = ring(4, -1)
    flip = ring(2, 1)
    below = lax.ppermute(own, "z", up)
    above = lax.ppermute(own, "z", down)
    side = lax.ppermute(own, "xl", flip)
    if early is not None:
        side, early = lax.optimization_barrier((side, early))
    far = lax.ppermute(below, "z", up)
    side_below = lax.ppermute(below, "xl", flip)
    side_above = lax.ppermute(side, "z", down)
    side_far_low = lax.ppermute(side_below[:half], "z", up)
    side_far_high = lax.ppermute(side_above[half:], "z", down)
    pieces = (
        (0, 0, 0, own),
        (0, 3, 0, below),
        (0, 1, 0, above),
        (1, 0, 0, side),
        (1, 3, 0, side_below),
        (1, 1, 0, side_above),
        (0, 2, 0, far),
        (1, 2, 0, side_far_low),
        (1, 2, half, side_far_high),
    )
    return pieces, early


def place_of(dx, dz):
    xl = lax.axis_index("xl")
    z = lax.axis_index("z")
    return ((xl + dx) % 2) * 4 + (z + dz) % 4


def gather_rows(own, early):
    rows, width = own.shape
    out = set_down(own, place_of(0, 0), 0)
    pieces, early = gather_pieces(own, early)
    for dx, dz, start, piece in pieces[1:]:
        out = lax.dynamic_update_slice(out, piece, (place_of(dx, dz) * rows + start, 0))
    return out, early


def set_down(own, place, axis):
    def body(place_ref, own_ref, out_ref):
        out_ref[...] = own_ref[...]

    shape = list(own.shape)
    shape[axis] *= 8
    index = (lambda i, p: (p[0], 0)) if axis == 0 else (lambda i, p: (0, p[0]))
    return pl.pallas_call(
        body,
        grid_spec=pltpu.PrefetchScalarGridSpec(
            num_scalar_prefetch=1,
            grid=(1,),
            in_specs=[pl.BlockSpec(own.shape, lambda i, p: (0, 0))],
            out_specs=pl.BlockSpec(own.shape, index),
        ),
        out_shape=jax.ShapeDtypeStruct(shape, own.dtype),
        name="set_down",
    )(place.reshape(1), own)


def gather_columns(own):
    rows, width = own.shape
    out = set_down(own, place_of(0, 0), 1)
    for dx, dz, start, piece in gather_pieces(own)[0][1:]:
        out = lax.dynamic_update_slice(out, piece, (start, place_of(dx, dz) * width))
    return out


def swap_cores(values):
    return lax.ppermute(values, "c", [(0, 1), (1, 0)])


def attention(tokens_all, gain, w_latent, w_query, w_key_up, w_value_up, positions, request_table, block=512):
    rows, width = tokens_all.shape
    heads = w_query.shape[1] // HD
    blocks = rows // block

    def body(
        x_ref,
        gain_ref,
        wl_ref,
        wq_ref,
        wk_ref,
        wv_ref,
        pos_ref,
        table_ref,
        out_ref,
        lat_ref,
        ql_ref,
        marks_ref,
    ):
        phase = pl.program_id(0)
        start = pl.multiple_of(pl.program_id(1) * block, block)

        @pl.when((phase == 0) & (start == 0))
        def _():
            position = pos_ref[...].astype(f32)
            table = table_ref[...].astype(f32)
            request = jnp.zeros_like(position)
            for value in range(1, 4):
                first = jnp.sum((table < value).astype(f32), axis=1, keepdims=True)
                request = request + (position >= first).astype(f32)
            marks_ref[0:1, :] = position
            marks_ref[1:2, :] = request
            marks_ref[2:8, :] = jnp.zeros((6, rows), f32)

        @pl.when(phase == 0)
        def _():
            x = x_ref[...].astype(f32)
            mean_square = jnp.mean(x * x, axis=-1, keepdims=True)
            normed = (x * lax.rsqrt(mean_square + epsilon) * gain_ref[...].astype(f32)).astype(bf16)
            lat = jnp.dot(normed, wl_ref[...], preferred_element_type=f32)
            lat_ref[pl.ds(start, block), :] = lat.astype(bf16)
            queries = jnp.dot(normed, wq_ref[...], preferred_element_type=f32).astype(bf16)
            for head in range(heads):
                cols = slice(head * HD, (head + 1) * HD)
                ql = lax.dot_general(
                    queries[:, cols], wk_ref[:, cols], (((1,), (1,)), ((), ())), preferred_element_type=f32
                )
                ql_ref[head, pl.ds(start, block), :] = ql.astype(bf16)

        @pl.when(phase == 1)
        def _():
            lat = lat_ref[...]
            down = marks_ref[:, pl.ds(start, block)].T
            seen = (marks_ref[0:1, :] <= down[:, 0:1]) & (marks_ref[1:2, :] == down[:, 1:2])
            for head in range(heads):
                cols = slice(head * HD, (head + 1) * HD)
                ql = ql_ref[head, pl.ds(start, block), :]
                scores = lax.dot_general(
                    ql, lat, (((1,), (1,)), ((), ())), preferred_element_type=f32
                )
                scores = jnp.where(seen, scores, -1e30)
                largest = jnp.max(scores, axis=1, keepdims=True)
                raised = jnp.exp2((scores - largest) * exponent_scale)
                total = jnp.sum(raised, axis=1, keepdims=True)
                mixed = jnp.dot(raised.astype(bf16), lat, preferred_element_type=f32)
                mixed = (mixed * (1.0 / total)).astype(bf16)
                head_out = jnp.dot(mixed, wv_ref[:, cols], preferred_element_type=f32).astype(bf16)
                out_ref[:, cols] = head_out

    whole = lambda a: pl.BlockSpec(a.shape, lambda p, i: (0,) * a.ndim)
    late = lambda p, i: jnp.where(p == 0, 0, i)
    return pl.pallas_call(
        body,
        grid_spec=pl.GridSpec(
            grid=(2, blocks),
            in_specs=[
                pl.BlockSpec((block, width), lambda p, i: (jnp.where(p == 0, i, blocks - 1), 0)),
                whole(gain),
                whole(w_latent),
                whole(w_query),
                whole(w_key_up),
                whole(w_value_up),
                whole(positions),
                whole(request_table),
            ],
            out_specs=pl.BlockSpec((block, heads * HD), lambda p, i: (late(p, i), 0)),
            scratch_shapes=[
                pltpu.VMEM((rows, LAT), bf16),
                pltpu.VMEM((heads, rows, LAT), bf16),
                pltpu.VMEM((8, rows), f32),
            ],
        ),
        out_shape=jax.ShapeDtypeStruct((rows, heads * HD), bf16),
        compiler_params=pltpu.CompilerParams(
            dimension_semantics=("arbitrary", "arbitrary"), vmem_limit_bytes=62 * 1024 * 1024
        ),
        name="attend",
    )(
        tokens_all,
        gain,
        w_latent,
        w_query,
        w_key_up,
        w_value_up,
        positions,
        request_table,
    )


def run_dispatch(here, joined, own, w_out, gain, spread, together_of=4, slot_block=512):
    rows, width = own.shape
    pieces, inner, span = w_out.shape
    slots = spread.shape[0]
    first = pieces // together_of
    last = slots // slot_block

    def body(here_ref, j_ref, x_ref, wo_ref, gain_ref, spread_ref, resid_ref, out_ref, moe_ref):
        step = pl.program_id(0)

        @pl.when(step < first)
        def _():
            for part in range(together_of):
                start = (step * together_of + part) * span
                cols = pl.ds(pl.multiple_of(start, span), span)
                attended = jnp.dot(j_ref[...], wo_ref[part], preferred_element_type=f32)
                added = x_ref[:, cols].astype(f32) + attended
                resid_ref[:, cols] = added.astype(bf16)

        @pl.when(step == first)
        def _():
            resid = resid_ref[...].astype(f32)
            mean_square = jnp.mean(resid * resid, axis=-1, keepdims=True)
            normed = resid * lax.rsqrt(mean_square + epsilon) * gain_ref[...].astype(f32)
            moe_ref[...] = normed.astype(bf16)

        @pl.when(step >= first)
        def _():
            out_ref[...] = jnp.dot(
                spread_ref[...], moe_ref[...], preferred_element_type=f32
            ).astype(bf16)

    late = lambda i: jnp.maximum(i - first, 0)
    return pl.pallas_call(
        body,
        grid_spec=pltpu.PrefetchScalarGridSpec(
            num_scalar_prefetch=1,
            grid=(first + last,),
            in_specs=[
                pl.BlockSpec((rows, inner), lambda i, h: (h[0], 0)),
                pl.BlockSpec((rows, width), lambda i, h: (0, 0)),
                pl.BlockSpec(
                    (together_of, inner, span), lambda i, h: (jnp.minimum(i, first - 1), 0, 0)
                ),
                pl.BlockSpec((1, width), lambda i, h: (0, 0)),
                pl.BlockSpec((slot_block, rows), lambda i, h: (late(i), 0)),
            ],
            out_specs=[
                pl.BlockSpec((rows, width), lambda i, h: (0, 0)),
                pl.BlockSpec((slot_block, width), lambda i, h: (late(i), 0)),
            ],
            scratch_shapes=[pltpu.VMEM((rows, width), bf16)],
        ),
        out_shape=[
            jax.ShapeDtypeStruct((rows, width), bf16),
            jax.ShapeDtypeStruct((slots, width), bf16),
        ],
        compiler_params=pltpu.CompilerParams(
            dimension_semantics=("arbitrary",), vmem_limit_bytes=58 * 1024 * 1024
        ),
        name="dispatch",
    )(here.reshape(1), joined, own, w_out, gain, spread)


def run_combine(mixing, returned, resid, shared_out, block=512):
    rows, width = resid.shape

    def body(m_ref, r_ref, resid_ref, shared_ref, out_ref):
        parts = jnp.dot(m_ref[...], r_ref[...], preferred_element_type=f32)
        routed = parts[:rows] + parts[rows : 2 * rows] + parts[2 * rows :]
        total = resid_ref[...].astype(f32) + shared_ref[...].astype(f32) + routed
        out_ref[...] = total.astype(bf16)

    by_cols = lambda a: pl.BlockSpec((a.shape[0], block), lambda i: (0, i))
    return pl.pallas_call(
        body,
        grid=(width // block,),
        in_specs=[
            pl.BlockSpec(mixing.shape, lambda i: (0, 0)),
            by_cols(returned),
            by_cols(resid),
            by_cols(shared_out),
        ],
        out_specs=by_cols(resid),
        out_shape=jax.ShapeDtypeStruct((rows, width), bf16),
        compiler_params=pltpu.CompilerParams(
            dimension_semantics=("arbitrary",), vmem_limit_bytes=58 * 1024 * 1024
        ),
        name="combine",
    )(mixing, returned, resid, shared_out)


def run_shared(joined, tokens_all, w_out, gain, w_gate, w_up, w_down, block=256):
    rows, width = tokens_all.shape
    pieces, _, span = w_out.shape

    def body(j_ref, x_ref, wo_ref, gain_ref, wg_ref, wu_ref, wd_ref, out_ref, res_ref):
        for piece in range(pieces):
            cols = slice(piece * span, (piece + 1) * span)
            attended = jnp.dot(j_ref[...], wo_ref[piece], preferred_element_type=f32)
            added = x_ref[:, cols].astype(f32) + attended
            res_ref[:, cols] = added.astype(bf16)
        resid = res_ref[...].astype(f32)
        mean_square = jnp.mean(resid * resid, axis=-1, keepdims=True)
        moe_in = (resid * lax.rsqrt(mean_square + epsilon) * gain_ref[...].astype(f32)).astype(bf16)
        across = (((1,), (1,)), ((), ()))
        gate = lax.dot_general(moe_in, wg_ref[...], across, preferred_element_type=f32)
        up = lax.dot_general(moe_in, wu_ref[...], across, preferred_element_type=f32)
        act = (gate * (1.0 / (1.0 + jnp.exp(-gate))) * up).astype(bf16)
        out_ref[...] = jnp.dot(act, wd_ref[...], preferred_element_type=f32).astype(bf16)

    whole = lambda a: pl.BlockSpec(a.shape, lambda i: (0,) * a.ndim)
    by_rows = lambda a: pl.BlockSpec((block, a.shape[1]), lambda i: (i, 0))
    operands = (joined, tokens_all, w_out, gain, w_gate, w_up, w_down)
    return pl.pallas_call(
        body,
        grid=(rows // block,),
        in_specs=[by_rows(joined), by_rows(tokens_all)] + [whole(a) for a in operands[2:]],
        out_specs=by_rows(tokens_all),
        out_shape=jax.ShapeDtypeStruct((rows, width), bf16),
        scratch_shapes=[pltpu.VMEM((block, width), bf16)],
        compiler_params=pltpu.CompilerParams(
            dimension_semantics=("arbitrary",), vmem_limit_bytes=58 * 1024 * 1024
        ),
        cost_estimate=pl.CostEstimate(
            flops=13_000_000_000, bytes_accessed=25_000_000, transcendentals=720_000
        ),
        name="shared",
    )(*operands)


def at_row(start, block):
    return start if isinstance(start, int) else pl.multiple_of(start, block)


def run_experts(x, weights, block=256):
    rows, width = x.shape
    hidden = weights[0].shape[0]
    blocks = rows // block

    def body(x_hbm, g0, u0, d0, g1, u1, d1, out_hbm, xs, outs, gs, us, ds, x_sems, w_sems, out_sems):
        def load_x(i):
            at = pl.ds(at_row(i * block, block), block)
            return pltpu.make_async_copy(x_hbm.at[at], xs.at[at], x_sems.at[i])

        def save(i):
            at = pl.ds(at_row(i * block, block), block)
            return pltpu.make_async_copy(outs.at[at], out_hbm.at[at], out_sems.at[i])

        loads = []
        for half, (g, u, d) in enumerate(((g0, u0, d0), (g1, u1, d1))):
            loads.append(
                (
                    pltpu.make_async_copy(g, gs.at[half], w_sems.at[half, 0]),
                    pltpu.make_async_copy(u, us.at[half], w_sems.at[half, 1]),
                    pltpu.make_async_copy(d, ds.at[half], w_sems.at[half, 2]),
                )
            )
        load_x(0).start()
        for one in loads[0]:
            one.start()
        for i in range(1, blocks):
            load_x(i).start()
        for one in loads[1]:
            one.start()
        across = (((1,), (1,)), ((), ()))
        for half in range(2):

            def step(i, carry, waits):
                at = pl.ds(at_row(i * block, block), block)
                if half == 0:
                    load_x(i).wait()
                if waits:
                    loads[half][0].wait()
                xb = xs[at, :]
                gate = lax.dot_general(xb, gs[half], across, preferred_element_type=f32)
                if waits:
                    loads[half][1].wait()
                up = lax.dot_general(xb, us[half], across, preferred_element_type=f32)
                act = (gate * (1.0 / (1.0 + jnp.exp(-gate))) * up).astype(bf16)
                if waits:
                    loads[half][2].wait()
                res = jnp.dot(act, ds[half], preferred_element_type=f32).astype(bf16)
                if half == 0:
                    outs[at, :] = res
                else:
                    outs[at, :] = (outs[at, :].astype(f32) + res.astype(f32)).astype(bf16)
                    save(i).start()
                return carry

            step(0, 0, True)
            lax.fori_loop(1, blocks, lambda i, carry: step(i, carry, False), 0)
        for i in range(blocks):
            save(i).wait()

    hbm = pl.BlockSpec(memory_space=pl.ANY)
    return pl.pallas_call(
        body,
        in_specs=[hbm] * 7,
        out_specs=hbm,
        out_shape=jax.ShapeDtypeStruct((rows, width), bf16),
        scratch_shapes=[
            pltpu.VMEM((rows, width), bf16),
            pltpu.VMEM((rows, width), bf16),
            pltpu.VMEM((2, hidden, width), bf16),
            pltpu.VMEM((2, hidden, width), bf16),
            pltpu.VMEM((2, hidden, width), bf16),
            pltpu.SemaphoreType.DMA((blocks,)),
            pltpu.SemaphoreType.DMA((2, 3)),
            pltpu.SemaphoreType.DMA((blocks,)),
        ],
        compiler_params=pltpu.CompilerParams(vmem_limit_bytes=60 * 1024 * 1024),
        cost_estimate=pl.CostEstimate(
            flops=17_700_000_000, bytes_accessed=30_000_000, transcendentals=1_500_000
        ),
        name="experts",
    )(x, *weights)


def routing_tables(ids, gates, experts=64):
    top, rows = ids.shape
    slots = experts * CAP

    def body(ids_ref, gates_ref, spread_ref, mixing_ref):
        expert = lax.broadcasted_iota(jnp.int32, (experts, rows), 0)
        chosen = jnp.zeros((experts, rows), f32)
        gate_of = jnp.zeros((experts, rows), f32)
        for route in range(top):
            named = ids_ref[route : route + 1, :] == expert
            chosen = jnp.where(named, 1.0, chosen)
            gate_of = jnp.where(named, gates_ref[route : route + 1, :], gate_of)
        line = lax.broadcasted_iota(jnp.int32, (rows, rows), 0)
        before = (line < lax.broadcasted_iota(jnp.int32, (rows, rows), 1)).astype(f32).astype(bf16)
        earlier = jnp.dot(chosen.astype(bf16), before, preferred_element_type=f32)
        slot = jnp.where(chosen > 0.0, earlier, -1.0)

        owner = lax.broadcasted_iota(jnp.int32, (slots, experts), 0) // CAP
        owned = owner == lax.broadcasted_iota(jnp.int32, (slots, experts), 1)
        repeat = owned.astype(f32).astype(bf16)
        number = (lax.broadcasted_iota(jnp.int32, (slots, rows), 0) % CAP).astype(f32)
        tall = jnp.dot(repeat, slot.astype(bf16), preferred_element_type=f32)
        spread_ref[...] = (tall == number).astype(f32).astype(bf16)

        owner = lax.broadcasted_iota(jnp.int32, (experts, slots), 1) // CAP
        owned = owner == lax.broadcasted_iota(jnp.int32, (experts, slots), 0)
        repeat = owned.astype(f32).astype(bf16)
        number = (lax.broadcasted_iota(jnp.int32, (rows, slots), 1) % CAP).astype(f32)
        wide = jnp.dot(slot.T.astype(bf16), repeat, preferred_element_type=f32)
        hit = wide == number
        rest = gate_of.T
        for part in range(3):
            now = rest.astype(bf16)
            rest = rest - now.astype(f32)
            weights = jnp.dot(now, repeat, preferred_element_type=f32)
            mixing_ref[part * rows : (part + 1) * rows, :] = jnp.where(hit, weights, 0.0).astype(bf16)

    return pl.pallas_call(
        body,
        out_shape=[
            jax.ShapeDtypeStruct((slots, rows), bf16),
            jax.ShapeDtypeStruct((3 * rows, slots), bf16),
        ],
        name="routing",
    )(ids, gates)


def shards(
    tokens,
    position_of_row,
    request_of_position,
    expert_ids,
    gate_values,
    attn_norm,
    moe_norm,
    w_query,
    w_latent,
    w_key_up,
    w_value_up,
    w_output,
    w_shared_gate,
    w_shared_up,
    w_shared_down,
    w_routed_gate,
    w_routed_up,
    w_routed_down,
):
    own = tokens[0]
    rows, width = own.shape
    here = place_of(0, 0)
    core = lax.axis_index("c")

    spread, mixing = routing_tables(expert_ids[0].T, gate_values[0].T)

    span = w_output.shape[1] // 8
    block_here = lax.axis_index("y") * 2 + core
    columns = lax.dynamic_slice(w_output, (0, block_here * span), (w_output.shape[0], span))
    columns = lax.all_gather(columns, SEQ, axis=0, tiled=True)

    early = (spread, mixing, attn_norm.reshape(1, -1), moe_norm.reshape(1, -1))
    tokens_all, (spread, mixing, attn_gain, moe_gain) = gather_rows(own, early)

    own_half = (w_routed_gate[0].T, w_routed_up[0].T, w_routed_down[0])
    columns, own_half, tokens_all = lax.optimization_barrier((columns, own_half, tokens_all))
    other_half = tuple(swap_cores(w) for w in own_half)
    w_out = lax.all_gather(columns, ("y", "c"), axis=0, tiled=False)

    head_out = attention(
        tokens_all,
        attn_gain,
        w_latent,
        w_query,
        w_key_up,
        w_value_up,
        position_of_row,
        request_of_position,
    )
    head_out, other_half = lax.optimization_barrier((head_out, other_half))
    joined = gather_columns(head_out)

    resid, outgoing = run_dispatch(here, joined, own, w_out, moe_gain, spread)
    outgoing, joined = lax.optimization_barrier((outgoing, joined))
    slots = outgoing.shape[0]
    arrived = lax.all_to_all(
        outgoing.reshape(128, slots // 128, width), ALL, split_axis=0, concat_axis=0, tiled=True
    ).reshape(slots, width)

    shared_part = run_shared(
        joined,
        tokens_all,
        w_out,
        moe_gain,
        w_shared_gate.T,
        w_shared_up.T,
        w_shared_down,
    )
    arrived, _ = lax.optimization_barrier((arrived, shared_part))
    shared_out = lax.psum_scatter(
        shared_part,
        SEQ,
        scatter_dimension=0,
        tiled=True,
    )

    expert_out = run_experts(arrived, own_half + other_half)
    returned = lax.all_to_all(
        expert_out.reshape(128, slots // 128, width), ALL, split_axis=0, concat_axis=0, tiled=True
    ).reshape(slots, width)
    layer_out = run_combine(mixing, returned, resid, shared_out)
    return layer_out.reshape(1, rows, width)


def solution(mesh):
    fine = Mesh(mesh.devices.reshape(2, 4, 2, 4, 2), ALL)
    in_specs = (
        P(EXP, SEQ, None),
        P(EXP, None),
        P(EXP, None),
        P(EXP, SEQ, None),
        P(EXP, SEQ, None),
        P(),
        P(),
        P(None, SEQ),
        P(),
        P(None, SEQ),
        P(None, SEQ),
        P(SEQ, None),
        P(None, SEQ),
        P(None, SEQ),
        P(SEQ, None),
        P(ALL, None, None),
        P(ALL, None, None),
        P(ALL, None, None),
    )
    out_specs = P(EXP, SEQ, None)
    return jax.shard_map(shards, mesh=fine, in_specs=in_specs, out_specs=out_specs, check_vma=False)
```

```python
import jax
import jax.numpy as jnp
from jax import lax
from jax.experimental import pallas as pl
from jax.experimental.pallas import tpu as pltpu
from jax.sharding import Mesh
from jax.sharding import PartitionSpec as P

HD = 128
LAT = 512
CAP = 16

SEQ = ("xl", "z")
EXP = ("xh", "y", "c")
ALL = SEQ + EXP

epsilon = 1e-06
exponent_scale = 192.0 ** (-0.5) * 1.4426950408889634
f32 = jnp.float32
bf16 = jnp.bfloat16


def ring(count, step):
    return [(i, (i + step) % count) for i in range(count)]


def gather_pieces(own, early=None):
    half = own.shape[0] // 2
    up = ring(4, 1)
    down = ring(4, -1)
    flip = ring(2, 1)
    below = lax.ppermute(own, "z", up)
    above = lax.ppermute(own, "z", down)
    side = lax.ppermute(own, "xl", flip)
    if early is not None:
        side, early = lax.optimization_barrier((side, early))
    far = lax.ppermute(below, "z", up)
    side_below = lax.ppermute(below, "xl", flip)
    side_above = lax.ppermute(side, "z", down)
    side_far_low = lax.ppermute(side_below[:half], "z", up)
    side_far_high = lax.ppermute(side_above[half:], "z", down)
    pieces = (
        (0, 0, 0, own),
        (0, 3, 0, below),
        (0, 1, 0, above),
        (1, 0, 0, side),
        (1, 3, 0, side_below),
        (1, 1, 0, side_above),
        (0, 2, 0, far),
        (1, 2, 0, side_far_low),
        (1, 2, half, side_far_high),
    )
    return pieces, early


def place_of(dx, dz):
    xl = lax.axis_index("xl")
    z = lax.axis_index("z")
    return ((xl + dx) % 2) * 4 + (z + dz) % 4


def gather_rows(own, early):
    rows, width = own.shape
    out = set_down(own, place_of(0, 0), 0)
    pieces, early = gather_pieces(own, early)
    for dx, dz, start, piece in pieces[1:]:
        out = lax.dynamic_update_slice(out, piece, (place_of(dx, dz) * rows + start, 0))
    return out, early


def set_down(own, place, axis):
    def body(place_ref, own_ref, out_ref):
        out_ref[...] = own_ref[...]

    shape = list(own.shape)
    shape[axis] *= 8
    index = (lambda i, p: (p[0], 0)) if axis == 0 else (lambda i, p: (0, p[0]))
    return pl.pallas_call(
        body,
        grid_spec=pltpu.PrefetchScalarGridSpec(
            num_scalar_prefetch=1,
            grid=(1,),
            in_specs=[pl.BlockSpec(own.shape, lambda i, p: (0, 0))],
            out_specs=pl.BlockSpec(own.shape, index),
        ),
        out_shape=jax.ShapeDtypeStruct(shape, own.dtype),
        name="set_down",
    )(place.reshape(1), own)


def gather_columns(own, early):
    rows, width = own.shape
    out = set_down(own, place_of(0, 0), 1)
    pieces, (early, out) = gather_pieces(own, (early, out))
    for dx, dz, start, piece in pieces[1:]:
        out = lax.dynamic_update_slice(out, piece, (start, place_of(dx, dz) * width))
    return out, early


def swap_cores(values):
    return lax.ppermute(values, "c", [(0, 1), (1, 0)])


def attention(tokens_all, gain, w_latent, w_query, w_key_up, w_value_up, positions, request_table, block=512):
    rows, width = tokens_all.shape
    heads = w_query.shape[1] // HD
    blocks = rows // block

    def body(
        x_ref,
        gain_ref,
        wl_ref,
        wq_ref,
        wk_ref,
        wv_ref,
        pos_ref,
        table_ref,
        out_ref,
        lat_ref,
        ql_ref,
        marks_ref,
    ):
        phase = pl.program_id(0)
        start = pl.multiple_of(pl.program_id(1) * block, block)

        @pl.when((phase == 0) & (start == 0))
        def _():
            position = pos_ref[...].astype(f32)
            table = table_ref[...].astype(f32)
            request = jnp.zeros_like(position)
            for value in range(1, 4):
                first = jnp.sum((table < value).astype(f32), axis=1, keepdims=True)
                request = request + (position >= first).astype(f32)
            marks_ref[0:1, :] = position
            marks_ref[1:2, :] = request
            marks_ref[2:8, :] = jnp.zeros((6, rows), f32)

        @pl.when(phase == 0)
        def _():
            x = x_ref[...].astype(f32)
            mean_square = jnp.mean(x * x, axis=-1, keepdims=True)
            normed = (x * lax.rsqrt(mean_square + epsilon) * gain_ref[...].astype(f32)).astype(bf16)
            lat = jnp.dot(normed, wl_ref[...], preferred_element_type=f32)
            lat_ref[pl.ds(start, block), :] = lat.astype(bf16)
            queries = jnp.dot(normed, wq_ref[...], preferred_element_type=f32).astype(bf16)
            for head in range(heads):
                cols = slice(head * HD, (head + 1) * HD)
                ql = lax.dot_general(
                    queries[:, cols], wk_ref[:, cols], (((1,), (1,)), ((), ())), preferred_element_type=f32
                )
                ql_ref[head, pl.ds(start, block), :] = ql.astype(bf16)

        @pl.when(phase == 1)
        def _():
            lat = lat_ref[...]
            down = marks_ref[:, pl.ds(start, block)].T
            seen = (marks_ref[0:1, :] <= down[:, 0:1]) & (marks_ref[1:2, :] == down[:, 1:2])
            for head in range(heads):
                cols = slice(head * HD, (head + 1) * HD)
                ql = ql_ref[head, pl.ds(start, block), :]
                scores = lax.dot_general(
                    ql, lat, (((1,), (1,)), ((), ())), preferred_element_type=f32
                )
                scores = jnp.where(seen, scores, -1e30)
                largest = jnp.max(scores, axis=1, keepdims=True)
                raised = jnp.exp2((scores - largest) * exponent_scale)
                total = jnp.sum(raised, axis=1, keepdims=True)
                mixed = jnp.dot(raised.astype(bf16), lat, preferred_element_type=f32)
                mixed = (mixed * (1.0 / total)).astype(bf16)
                head_out = jnp.dot(mixed, wv_ref[:, cols], preferred_element_type=f32).astype(bf16)
                out_ref[:, cols] = head_out

    whole = lambda a: pl.BlockSpec(a.shape, lambda p, i: (0,) * a.ndim)
    late = lambda p, i: jnp.where(p == 0, 0, i)
    return pl.pallas_call(
        body,
        grid_spec=pl.GridSpec(
            grid=(2, blocks),
            in_specs=[
                pl.BlockSpec((block, width), lambda p, i: (jnp.where(p == 0, i, blocks - 1), 0)),
                whole(gain),
                whole(w_latent),
                whole(w_query),
                whole(w_key_up),
                whole(w_value_up),
                whole(positions),
                whole(request_table),
            ],
            out_specs=pl.BlockSpec((block, heads * HD), lambda p, i: (late(p, i), 0)),
            scratch_shapes=[
                pltpu.VMEM((rows, LAT), bf16),
                pltpu.VMEM((heads, rows, LAT), bf16),
                pltpu.VMEM((8, rows), f32),
            ],
        ),
        out_shape=jax.ShapeDtypeStruct((rows, heads * HD), bf16),
        compiler_params=pltpu.CompilerParams(
            dimension_semantics=("arbitrary", "arbitrary"), vmem_limit_bytes=62 * 1024 * 1024
        ),
        name="attend",
    )(
        tokens_all,
        gain,
        w_latent,
        w_query,
        w_key_up,
        w_value_up,
        positions,
        request_table,
    )


def run_dispatch(here, joined, own, w_out, gain, spread, together_of=4, slot_block=512):
    rows, width = own.shape
    pieces, inner, span = w_out.shape
    slots = spread.shape[0]
    first = pieces // together_of
    last = slots // slot_block

    def body(here_ref, j_ref, x_ref, wo_ref, gain_ref, spread_ref, resid_ref, out_ref, moe_ref):
        step = pl.program_id(0)

        @pl.when(step < first)
        def _():
            for part in range(together_of):
                start = (step * together_of + part) * span
                cols = pl.ds(pl.multiple_of(start, span), span)
                attended = jnp.dot(j_ref[...], wo_ref[part], preferred_element_type=f32)
                added = x_ref[:, cols].astype(f32) + attended
                resid_ref[:, cols] = added.astype(bf16)

        @pl.when(step == first)
        def _():
            resid = resid_ref[...].astype(f32)
            mean_square = jnp.mean(resid * resid, axis=-1, keepdims=True)
            normed = resid * lax.rsqrt(mean_square + epsilon) * gain_ref[...].astype(f32)
            moe_ref[...] = normed.astype(bf16)

        @pl.when(step >= first)
        def _():
            out_ref[...] = jnp.dot(
                spread_ref[...], moe_ref[...], preferred_element_type=f32
            ).astype(bf16)

    late = lambda i: jnp.maximum(i - first, 0)
    return pl.pallas_call(
        body,
        grid_spec=pltpu.PrefetchScalarGridSpec(
            num_scalar_prefetch=1,
            grid=(first + last,),
            in_specs=[
                pl.BlockSpec((rows, inner), lambda i, h: (h[0], 0)),
                pl.BlockSpec((rows, width), lambda i, h: (0, 0)),
                pl.BlockSpec(
                    (together_of, inner, span), lambda i, h: (jnp.minimum(i, first - 1), 0, 0)
                ),
                pl.BlockSpec((1, width), lambda i, h: (0, 0)),
                pl.BlockSpec((slot_block, rows), lambda i, h: (late(i), 0)),
            ],
            out_specs=[
                pl.BlockSpec((rows, width), lambda i, h: (0, 0)),
                pl.BlockSpec((slot_block, width), lambda i, h: (late(i), 0)),
            ],
            scratch_shapes=[pltpu.VMEM((rows, width), bf16)],
        ),
        out_shape=[
            jax.ShapeDtypeStruct((rows, width), bf16),
            jax.ShapeDtypeStruct((slots, width), bf16),
        ],
        compiler_params=pltpu.CompilerParams(
            dimension_semantics=("arbitrary",), vmem_limit_bytes=58 * 1024 * 1024
        ),
        name="dispatch",
    )(here.reshape(1), joined, own, w_out, gain, spread)


def run_combine(mixing, returned, resid, shared_out, block=512):
    rows, width = resid.shape

    def body(m_ref, r_ref, resid_ref, shared_ref, out_ref):
        parts = jnp.dot(m_ref[...], r_ref[...], preferred_element_type=f32)
        routed = parts[:rows] + parts[rows : 2 * rows] + parts[2 * rows :]
        total = resid_ref[...].astype(f32) + shared_ref[...].astype(f32) + routed
        out_ref[...] = total.astype(bf16)

    by_cols = lambda a: pl.BlockSpec((a.shape[0], block), lambda i: (0, i))
    return pl.pallas_call(
        body,
        grid=(width // block,),
        in_specs=[
            pl.BlockSpec(mixing.shape, lambda i: (0, 0)),
            by_cols(returned),
            by_cols(resid),
            by_cols(shared_out),
        ],
        out_specs=by_cols(resid),
        out_shape=jax.ShapeDtypeStruct((rows, width), bf16),
        compiler_params=pltpu.CompilerParams(
            dimension_semantics=("arbitrary",), vmem_limit_bytes=58 * 1024 * 1024
        ),
        name="combine",
    )(mixing, returned, resid, shared_out)


def run_shared(joined, tokens_all, w_out, gain, w_gate, w_up, w_down, block=256):
    rows, width = tokens_all.shape
    pieces, _, span = w_out.shape

    def body(j_ref, x_ref, wo_ref, gain_ref, wg_ref, wu_ref, wd_ref, out_ref, res_ref):
        for piece in range(pieces):
            cols = slice(piece * span, (piece + 1) * span)
            attended = jnp.dot(j_ref[...], wo_ref[piece], preferred_element_type=f32)
            added = x_ref[:, cols].astype(f32) + attended
            res_ref[:, cols] = added.astype(bf16)
        resid = res_ref[...].astype(f32)
        mean_square = jnp.mean(resid * resid, axis=-1, keepdims=True)
        moe_in = (resid * lax.rsqrt(mean_square + epsilon) * gain_ref[...].astype(f32)).astype(bf16)
        across = (((1,), (1,)), ((), ()))
        gate = lax.dot_general(moe_in, wg_ref[...], across, preferred_element_type=f32)
        up = lax.dot_general(moe_in, wu_ref[...], across, preferred_element_type=f32)
        act = (gate * (1.0 / (1.0 + jnp.exp(-gate))) * up).astype(bf16)
        out_ref[...] = jnp.dot(act, wd_ref[...], preferred_element_type=f32).astype(bf16)

    whole = lambda a: pl.BlockSpec(a.shape, lambda i: (0,) * a.ndim)
    by_rows = lambda a: pl.BlockSpec((block, a.shape[1]), lambda i: (i, 0))
    operands = (joined, tokens_all, w_out, gain, w_gate, w_up, w_down)
    return pl.pallas_call(
        body,
        grid=(rows // block,),
        in_specs=[by_rows(joined), by_rows(tokens_all)] + [whole(a) for a in operands[2:]],
        out_specs=by_rows(tokens_all),
        out_shape=jax.ShapeDtypeStruct((rows, width), bf16),
        scratch_shapes=[pltpu.VMEM((block, width), bf16)],
        compiler_params=pltpu.CompilerParams(
            dimension_semantics=("arbitrary",), vmem_limit_bytes=58 * 1024 * 1024
        ),
        cost_estimate=pl.CostEstimate(
            flops=13_000_000_000, bytes_accessed=25_000_000, transcendentals=720_000
        ),
        name="shared",
    )(*operands)


def at_row(start, block):
    return start if isinstance(start, int) else pl.multiple_of(start, block)


def run_experts(x, weights, block=256):
    rows, width = x.shape
    hidden = weights[0].shape[0]
    blocks = rows // block

    def body(x_hbm, g0, u0, d0, g1, u1, d1, out_hbm, xs, outs, gs, us, ds, x_sems, w_sems, out_sems):
        def load_x(i):
            at = pl.ds(at_row(i * block, block), block)
            return pltpu.make_async_copy(x_hbm.at[at], xs.at[at], x_sems.at[i])

        def save(i):
            at = pl.ds(at_row(i * block, block), block)
            return pltpu.make_async_copy(outs.at[at], out_hbm.at[at], out_sems.at[i])

        loads = []
        for half, (g, u, d) in enumerate(((g0, u0, d0), (g1, u1, d1))):
            loads.append(
                (
                    pltpu.make_async_copy(g, gs.at[half], w_sems.at[half, 0]),
                    pltpu.make_async_copy(u, us.at[half], w_sems.at[half, 1]),
                    pltpu.make_async_copy(d, ds.at[half], w_sems.at[half, 2]),
                )
            )
        load_x(0).start()
        for one in loads[0]:
            one.start()
        for i in range(1, blocks):
            load_x(i).start()
        for one in loads[1]:
            one.start()
        across = (((1,), (1,)), ((), ()))
        for half in range(2):

            def step(i, carry, waits):
                at = pl.ds(at_row(i * block, block), block)
                if half == 0:
                    load_x(i).wait()
                if waits:
                    loads[half][0].wait()
                xb = xs[at, :]
                gate = lax.dot_general(xb, gs[half], across, preferred_element_type=f32)
                if waits:
                    loads[half][1].wait()
                up = lax.dot_general(xb, us[half], across, preferred_element_type=f32)
                act = (gate * (1.0 / (1.0 + jnp.exp(-gate))) * up).astype(bf16)
                if waits:
                    loads[half][2].wait()
                res = jnp.dot(act, ds[half], preferred_element_type=f32).astype(bf16)
                if half == 0:
                    outs[at, :] = res
                else:
                    outs[at, :] = (outs[at, :].astype(f32) + res.astype(f32)).astype(bf16)
                    save(i).start()
                return carry

            step(0, 0, True)
            lax.fori_loop(1, blocks, lambda i, carry: step(i, carry, False), 0)
        for i in range(blocks):
            save(i).wait()

    hbm = pl.BlockSpec(memory_space=pl.ANY)
    return pl.pallas_call(
        body,
        in_specs=[hbm] * 7,
        out_specs=hbm,
        out_shape=jax.ShapeDtypeStruct((rows, width), bf16),
        scratch_shapes=[
            pltpu.VMEM((rows, width), bf16),
            pltpu.VMEM((rows, width), bf16),
            pltpu.VMEM((2, hidden, width), bf16),
            pltpu.VMEM((2, hidden, width), bf16),
            pltpu.VMEM((2, hidden, width), bf16),
            pltpu.SemaphoreType.DMA((blocks,)),
            pltpu.SemaphoreType.DMA((2, 3)),
            pltpu.SemaphoreType.DMA((blocks,)),
        ],
        compiler_params=pltpu.CompilerParams(vmem_limit_bytes=60 * 1024 * 1024),
        cost_estimate=pl.CostEstimate(
            flops=17_700_000_000, bytes_accessed=30_000_000, transcendentals=1_500_000
        ),
        name="experts",
    )(x, *weights)


def routing_tables(ids, gates, experts=64):
    top, rows = ids.shape
    slots = experts * CAP

    def body(ids_ref, gates_ref, spread_ref, mixing_ref):
        expert = lax.broadcasted_iota(jnp.int32, (experts, rows), 0)
        chosen = jnp.zeros((experts, rows), f32)
        gate_of = jnp.zeros((experts, rows), f32)
        for route in range(top):
            named = ids_ref[route : route + 1, :] == expert
            chosen = jnp.where(named, 1.0, chosen)
            gate_of = jnp.where(named, gates_ref[route : route + 1, :], gate_of)
        line = lax.broadcasted_iota(jnp.int32, (rows, rows), 0)
        before = (line < lax.broadcasted_iota(jnp.int32, (rows, rows), 1)).astype(f32).astype(bf16)
        earlier = jnp.dot(chosen.astype(bf16), before, preferred_element_type=f32)
        slot = jnp.where(chosen > 0.0, earlier, -1.0)

        owner = lax.broadcasted_iota(jnp.int32, (slots, experts), 0) // CAP
        owned = owner == lax.broadcasted_iota(jnp.int32, (slots, experts), 1)
        repeat = owned.astype(f32).astype(bf16)
        number = (lax.broadcasted_iota(jnp.int32, (slots, rows), 0) % CAP).astype(f32)
        tall = jnp.dot(repeat, slot.astype(bf16), preferred_element_type=f32)
        spread_ref[...] = (tall == number).astype(f32).astype(bf16)

        owner = lax.broadcasted_iota(jnp.int32, (experts, slots), 1) // CAP
        owned = owner == lax.broadcasted_iota(jnp.int32, (experts, slots), 0)
        repeat = owned.astype(f32).astype(bf16)
        number = (lax.broadcasted_iota(jnp.int32, (rows, slots), 1) % CAP).astype(f32)
        wide = jnp.dot(slot.T.astype(bf16), repeat, preferred_element_type=f32)
        hit = wide == number
        rest = gate_of.T
        for part in range(3):
            now = rest.astype(bf16)
            rest = rest - now.astype(f32)
            weights = jnp.dot(now, repeat, preferred_element_type=f32)
            mixing_ref[part * rows : (part + 1) * rows, :] = jnp.where(hit, weights, 0.0).astype(bf16)

    return pl.pallas_call(
        body,
        out_shape=[
            jax.ShapeDtypeStruct((slots, rows), bf16),
            jax.ShapeDtypeStruct((3 * rows, slots), bf16),
        ],
        name="routing",
    )(ids, gates)


def shards(
    tokens,
    position_of_row,
    request_of_position,
    expert_ids,
    gate_values,
    attn_norm,
    moe_norm,
    w_query,
    w_latent,
    w_key_up,
    w_value_up,
    w_output,
    w_shared_gate,
    w_shared_up,
    w_shared_down,
    w_routed_gate,
    w_routed_up,
    w_routed_down,
):
    own = tokens[0]
    rows, width = own.shape
    here = place_of(0, 0)
    core = lax.axis_index("c")

    spread, mixing = routing_tables(expert_ids[0].T, gate_values[0].T)

    span = w_output.shape[1] // 8
    block_here = lax.axis_index("y") * 2 + core
    columns = lax.dynamic_slice(w_output, (0, block_here * span), (w_output.shape[0], span))
    columns = lax.all_gather(columns, SEQ, axis=0, tiled=True)

    tokens_all, attn_gain = gather_rows(own, attn_norm.reshape(1, -1))

    own_half = (w_routed_gate[0].T, w_routed_up[0].T, w_routed_down[0])
    columns, own_half, tokens_all = lax.optimization_barrier((columns, own_half, tokens_all))
    other_half = tuple(swap_cores(w) for w in own_half)
    w_out = lax.all_gather(columns, ("y", "c"), axis=0, tiled=False)

    head_out = attention(
        tokens_all,
        attn_gain,
        w_latent,
        w_query,
        w_key_up,
        w_value_up,
        position_of_row,
        request_of_position,
    )
    head_out, other_half = lax.optimization_barrier((head_out, other_half))
    early = (spread, mixing, moe_norm.reshape(1, -1))
    joined, (spread, mixing, moe_gain) = gather_columns(head_out, early)

    resid, outgoing = run_dispatch(here, joined, own, w_out, moe_gain, spread)
    outgoing, joined = lax.optimization_barrier((outgoing, joined))
    slots = outgoing.shape[0]
    arrived = lax.all_to_all(
        outgoing.reshape(128, slots // 128, width), ALL, split_axis=0, concat_axis=0, tiled=True
    ).reshape(slots, width)

    shared_part = run_shared(
        joined,
        tokens_all,
        w_out,
        moe_gain,
        w_shared_gate.T,
        w_shared_up.T,
        w_shared_down,
    )
    arrived, _ = lax.optimization_barrier((arrived, shared_part))
    shared_out = lax.psum_scatter(
        shared_part,
        SEQ,
        scatter_dimension=0,
        tiled=True,
    )

    expert_out = run_experts(arrived, own_half + other_half)
    returned = lax.all_to_all(
        expert_out.reshape(128, slots // 128, width), ALL, split_axis=0, concat_axis=0, tiled=True
    ).reshape(slots, width)
    layer_out = run_combine(mixing, returned, resid, shared_out)
    return layer_out.reshape(1, rows, width)


def solution(mesh):
    fine = Mesh(mesh.devices.reshape(2, 4, 2, 4, 2), ALL)
    in_specs = (
        P(EXP, SEQ, None),
        P(EXP, None),
        P(EXP, None),
        P(EXP, SEQ, None),
        P(EXP, SEQ, None),
        P(),
        P(),
        P(None, SEQ),
        P(),
        P(None, SEQ),
        P(None, SEQ),
        P(SEQ, None),
        P(None, SEQ),
        P(None, SEQ),
        P(SEQ, None),
        P(ALL, None, None),
        P(ALL, None, None),
        P(ALL, None, None),
    )
    out_specs = P(EXP, SEQ, None)
    return jax.shard_map(shards, mesh=fine, in_specs=in_specs, out_specs=out_specs, check_vma=False)
```

```python
import jax
import jax.numpy as jnp
from jax import lax
from jax.experimental import pallas as pl
from jax.experimental.pallas import tpu as pltpu
from jax.sharding import Mesh
from jax.sharding import PartitionSpec as P

HD = 128
LAT = 512
CAP = 16

SEQ = ("xl", "z")
EXP = ("xh", "y", "c")
ALL = SEQ + EXP

epsilon = 1e-06
exponent_scale = 192.0 ** (-0.5) * 1.4426950408889634
f32 = jnp.float32
bf16 = jnp.bfloat16


def ring(count, step):
    return [(i, (i + step) % count) for i in range(count)]


def gather_pieces(own, early=None):
    half = own.shape[0] // 2
    up = ring(4, 1)
    down = ring(4, -1)
    flip = ring(2, 1)
    below = lax.ppermute(own, "z", up)
    above = lax.ppermute(own, "z", down)
    side = lax.ppermute(own, "xl", flip)
    if early is not None:
        side, early = lax.optimization_barrier((side, early))
    far = lax.ppermute(below, "z", up)
    side_below = lax.ppermute(below, "xl", flip)
    side_above = lax.ppermute(side, "z", down)
    side_far_low = lax.ppermute(side_below[:half], "z", up)
    side_far_high = lax.ppermute(side_above[half:], "z", down)
    pieces = (
        (0, 0, 0, own),
        (0, 3, 0, below),
        (0, 1, 0, above),
        (1, 0, 0, side),
        (1, 3, 0, side_below),
        (1, 1, 0, side_above),
        (0, 2, 0, far),
        (1, 2, 0, side_far_low),
        (1, 2, half, side_far_high),
    )
    return pieces, early


def place_of(dx, dz):
    xl = lax.axis_index("xl")
    z = lax.axis_index("z")
    return ((xl + dx) % 2) * 4 + (z + dz) % 4


def gather_rows(own, early):
    rows, width = own.shape
    out = set_down(own, place_of(0, 0), 0)
    pieces, early = gather_pieces(own, early)
    for dx, dz, start, piece in pieces[1:]:
        out = lax.dynamic_update_slice(out, piece, (place_of(dx, dz) * rows + start, 0))
    return out, early


def set_down(own, place, axis):
    def body(place_ref, own_ref, out_ref):
        out_ref[...] = own_ref[...]

    shape = list(own.shape)
    shape[axis] *= 8
    index = (lambda i, p: (p[0], 0)) if axis == 0 else (lambda i, p: (0, p[0]))
    return pl.pallas_call(
        body,
        grid_spec=pltpu.PrefetchScalarGridSpec(
            num_scalar_prefetch=1,
            grid=(1,),
            in_specs=[pl.BlockSpec(own.shape, lambda i, p: (0, 0))],
            out_specs=pl.BlockSpec(own.shape, index),
        ),
        out_shape=jax.ShapeDtypeStruct(shape, own.dtype),
        name="set_down",
    )(place.reshape(1), own)


def gather_columns(own):
    rows, width = own.shape
    out = set_down(own, place_of(0, 0), 1)
    for dx, dz, start, piece in gather_pieces(own)[0][1:]:
        out = lax.dynamic_update_slice(out, piece, (start, place_of(dx, dz) * width))
    return out


def swap_cores(values):
    return lax.ppermute(values, "c", [(0, 1), (1, 0)])


def attention(tokens_all, gain, w_latent, w_query, w_key_up, w_value_up, positions, request_table, block=512):
    rows, width = tokens_all.shape
    heads = w_query.shape[1] // HD
    blocks = rows // block

    def body(
        x_ref,
        gain_ref,
        wl_ref,
        wq_ref,
        wk_ref,
        wv_ref,
        pos_ref,
        table_ref,
        out_ref,
        lat_ref,
        ql_ref,
        marks_ref,
    ):
        phase = pl.program_id(0)
        start = pl.multiple_of(pl.program_id(1) * block, block)

        @pl.when((phase == 0) & (start == 0))
        def _():
            position = pos_ref[...].astype(f32)
            table = table_ref[...].astype(f32)
            request = jnp.zeros_like(position)
            for value in range(1, 4):
                first = jnp.sum((table < value).astype(f32), axis=1, keepdims=True)
                request = request + (position >= first).astype(f32)
            marks_ref[0:1, :] = position
            marks_ref[1:2, :] = request
            marks_ref[2:8, :] = jnp.zeros((6, rows), f32)

        @pl.when(phase == 0)
        def _():
            x = x_ref[...].astype(f32)
            mean_square = jnp.mean(x * x, axis=-1, keepdims=True)
            normed = (x * lax.rsqrt(mean_square + epsilon) * gain_ref[...].astype(f32)).astype(bf16)
            lat = jnp.dot(normed, wl_ref[...], preferred_element_type=f32)
            lat_ref[pl.ds(start, block), :] = lat.astype(bf16)
            queries = jnp.dot(normed, wq_ref[...], preferred_element_type=f32).astype(bf16)
            for head in range(heads):
                cols = slice(head * HD, (head + 1) * HD)
                ql = lax.dot_general(
                    queries[:, cols], wk_ref[:, cols], (((1,), (1,)), ((), ())), preferred_element_type=f32
                )
                ql_ref[head, pl.ds(start, block), :] = ql.astype(bf16)

        @pl.when(phase == 1)
        def _():
            lat = lat_ref[...]
            down = marks_ref[:, pl.ds(start, block)].T
            seen = (marks_ref[0:1, :] <= down[:, 0:1]) & (marks_ref[1:2, :] == down[:, 1:2])
            for head in range(heads):
                cols = slice(head * HD, (head + 1) * HD)
                ql = ql_ref[head, pl.ds(start, block), :]
                scores = lax.dot_general(
                    ql, lat, (((1,), (1,)), ((), ())), preferred_element_type=f32
                )
                scores = jnp.where(seen, scores, -1e30)
                largest = jnp.max(scores, axis=1, keepdims=True)
                raised = jnp.exp2((scores - largest) * exponent_scale)
                total = jnp.sum(raised, axis=1, keepdims=True)
                mixed = jnp.dot(raised.astype(bf16), lat, preferred_element_type=f32)
                mixed = (mixed * (1.0 / total)).astype(bf16)
                head_out = jnp.dot(mixed, wv_ref[:, cols], preferred_element_type=f32).astype(bf16)
                out_ref[:, cols] = head_out

    whole = lambda a: pl.BlockSpec(a.shape, lambda p, i: (0,) * a.ndim)
    late = lambda p, i: jnp.where(p == 0, 0, i)
    return pl.pallas_call(
        body,
        grid_spec=pl.GridSpec(
            grid=(2, blocks),
            in_specs=[
                pl.BlockSpec((block, width), lambda p, i: (jnp.where(p == 0, i, blocks - 1), 0)),
                whole(gain),
                whole(w_latent),
                whole(w_query),
                whole(w_key_up),
                whole(w_value_up),
                whole(positions),
                whole(request_table),
            ],
            out_specs=pl.BlockSpec((block, heads * HD), lambda p, i: (late(p, i), 0)),
            scratch_shapes=[
                pltpu.VMEM((rows, LAT), bf16),
                pltpu.VMEM((heads, rows, LAT), bf16),
                pltpu.VMEM((8, rows), f32),
            ],
        ),
        out_shape=jax.ShapeDtypeStruct((rows, heads * HD), bf16),
        compiler_params=pltpu.CompilerParams(
            dimension_semantics=("arbitrary", "arbitrary"), vmem_limit_bytes=62 * 1024 * 1024
        ),
        name="attend",
    )(
        tokens_all,
        gain,
        w_latent,
        w_query,
        w_key_up,
        w_value_up,
        positions,
        request_table,
    )


def run_dispatch(here, joined, own, w_out, gain, spread, together_of=4, slot_block=512):
    rows, width = own.shape
    pieces, inner, span = w_out.shape
    slots = spread.shape[0]
    first = pieces // together_of
    last = slots // slot_block

    def body(here_ref, j_ref, x_ref, wo_ref, gain_ref, spread_ref, resid_ref, out_ref, moe_ref):
        step = pl.program_id(0)

        @pl.when(step < first)
        def _():
            for part in range(together_of):
                start = (step * together_of + part) * span
                cols = pl.ds(pl.multiple_of(start, span), span)
                attended = jnp.dot(j_ref[...], wo_ref[part], preferred_element_type=f32)
                added = x_ref[:, cols].astype(f32) + attended
                resid_ref[:, cols] = added.astype(bf16)

        @pl.when(step == first)
        def _():
            resid = resid_ref[...].astype(f32)
            mean_square = jnp.mean(resid * resid, axis=-1, keepdims=True)
            normed = resid * lax.rsqrt(mean_square + epsilon) * gain_ref[...].astype(f32)
            moe_ref[...] = normed.astype(bf16)

        @pl.when(step >= first)
        def _():
            out_ref[...] = jnp.dot(
                spread_ref[...], moe_ref[...], preferred_element_type=f32
            ).astype(bf16)

    late = lambda i: jnp.maximum(i - first, 0)
    return pl.pallas_call(
        body,
        grid_spec=pltpu.PrefetchScalarGridSpec(
            num_scalar_prefetch=1,
            grid=(first + last,),
            in_specs=[
                pl.BlockSpec((rows, inner), lambda i, h: (h[0], 0)),
                pl.BlockSpec((rows, width), lambda i, h: (0, 0)),
                pl.BlockSpec(
                    (together_of, inner, span), lambda i, h: (jnp.minimum(i, first - 1), 0, 0)
                ),
                pl.BlockSpec((1, width), lambda i, h: (0, 0)),
                pl.BlockSpec((slot_block, rows), lambda i, h: (late(i), 0)),
            ],
            out_specs=[
                pl.BlockSpec((rows, width), lambda i, h: (0, 0)),
                pl.BlockSpec((slot_block, width), lambda i, h: (late(i), 0)),
            ],
            scratch_shapes=[pltpu.VMEM((rows, width), bf16)],
        ),
        out_shape=[
            jax.ShapeDtypeStruct((rows, width), bf16),
            jax.ShapeDtypeStruct((slots, width), bf16),
        ],
        compiler_params=pltpu.CompilerParams(
            dimension_semantics=("arbitrary",), vmem_limit_bytes=58 * 1024 * 1024
        ),
        name="dispatch",
    )(here.reshape(1), joined, own, w_out, gain, spread)


def run_combine(mixing, returned, resid, shared_out, block=1024):
    rows, width = resid.shape

    def body(m_ref, r_ref, resid_ref, shared_ref, out_ref):
        parts = jnp.dot(m_ref[...], r_ref[...], preferred_element_type=f32)
        routed = parts[:rows] + parts[rows : 2 * rows] + parts[2 * rows :]
        total = resid_ref[...].astype(f32) + shared_ref[...].astype(f32) + routed
        out_ref[...] = total.astype(bf16)

    by_cols = lambda a: pl.BlockSpec((a.shape[0], block), lambda i: (0, i))
    return pl.pallas_call(
        body,
        grid=(width // block,),
        in_specs=[
            pl.BlockSpec(mixing.shape, lambda i: (0, 0)),
            by_cols(returned),
            by_cols(resid),
            by_cols(shared_out),
        ],
        out_specs=by_cols(resid),
        out_shape=jax.ShapeDtypeStruct((rows, width), bf16),
        compiler_params=pltpu.CompilerParams(
            dimension_semantics=("arbitrary",), vmem_limit_bytes=58 * 1024 * 1024
        ),
        name="combine",
    )(mixing, returned, resid, shared_out)


def run_shared(joined, tokens_all, w_out, gain, w_gate, w_up, w_down, block=256):
    rows, width = tokens_all.shape
    pieces, _, span = w_out.shape

    def body(j_ref, x_ref, wo_ref, gain_ref, wg_ref, wu_ref, wd_ref, out_ref, res_ref):
        for piece in range(pieces):
            cols = slice(piece * span, (piece + 1) * span)
            attended = jnp.dot(j_ref[...], wo_ref[piece], preferred_element_type=f32)
            added = x_ref[:, cols].astype(f32) + attended
            res_ref[:, cols] = added.astype(bf16)
        resid = res_ref[...].astype(f32)
        mean_square = jnp.mean(resid * resid, axis=-1, keepdims=True)
        moe_in = (resid * lax.rsqrt(mean_square + epsilon) * gain_ref[...].astype(f32)).astype(bf16)
        across = (((1,), (1,)), ((), ()))
        gate = lax.dot_general(moe_in, wg_ref[...], across, preferred_element_type=f32)
        up = lax.dot_general(moe_in, wu_ref[...], across, preferred_element_type=f32)
        act = (gate * (1.0 / (1.0 + jnp.exp(-gate))) * up).astype(bf16)
        out_ref[...] = jnp.dot(act, wd_ref[...], preferred_element_type=f32).astype(bf16)

    whole = lambda a: pl.BlockSpec(a.shape, lambda i: (0,) * a.ndim)
    by_rows = lambda a: pl.BlockSpec((block, a.shape[1]), lambda i: (i, 0))
    operands = (joined, tokens_all, w_out, gain, w_gate, w_up, w_down)
    return pl.pallas_call(
        body,
        grid=(rows // block,),
        in_specs=[by_rows(joined), by_rows(tokens_all)] + [whole(a) for a in operands[2:]],
        out_specs=by_rows(tokens_all),
        out_shape=jax.ShapeDtypeStruct((rows, width), bf16),
        scratch_shapes=[pltpu.VMEM((block, width), bf16)],
        compiler_params=pltpu.CompilerParams(
            dimension_semantics=("arbitrary",), vmem_limit_bytes=58 * 1024 * 1024
        ),
        cost_estimate=pl.CostEstimate(
            flops=13_000_000_000, bytes_accessed=25_000_000, transcendentals=720_000
        ),
        name="shared",
    )(*operands)


def at_row(start, block):
    return start if isinstance(start, int) else pl.multiple_of(start, block)


def run_experts(x, weights, block=256):
    rows, width = x.shape
    hidden = weights[0].shape[0]
    blocks = rows // block

    def body(x_hbm, g0, u0, d0, g1, u1, d1, out_hbm, xs, outs, gs, us, ds, x_sems, w_sems, out_sems):
        def load_x(i):
            at = pl.ds(at_row(i * block, block), block)
            return pltpu.make_async_copy(x_hbm.at[at], xs.at[at], x_sems.at[i])

        def save(i):
            at = pl.ds(at_row(i * block, block), block)
            return pltpu.make_async_copy(outs.at[at], out_hbm.at[at], out_sems.at[i])

        loads = []
        for half, (g, u, d) in enumerate(((g0, u0, d0), (g1, u1, d1))):
            loads.append(
                (
                    pltpu.make_async_copy(g, gs.at[half], w_sems.at[half, 0]),
                    pltpu.make_async_copy(u, us.at[half], w_sems.at[half, 1]),
                    pltpu.make_async_copy(d, ds.at[half], w_sems.at[half, 2]),
                )
            )
        load_x(0).start()
        for one in loads[0]:
            one.start()
        for i in range(1, blocks):
            load_x(i).start()
        for one in loads[1]:
            one.start()
        across = (((1,), (1,)), ((), ()))
        for half in range(2):

            def step(i, carry, waits):
                at = pl.ds(at_row(i * block, block), block)
                if half == 0:
                    load_x(i).wait()
                if waits:
                    loads[half][0].wait()
                xb = xs[at, :]
                gate = lax.dot_general(xb, gs[half], across, preferred_element_type=f32)
                if waits:
                    loads[half][1].wait()
                up = lax.dot_general(xb, us[half], across, preferred_element_type=f32)
                act = (gate * (1.0 / (1.0 + jnp.exp(-gate))) * up).astype(bf16)
                if waits:
                    loads[half][2].wait()
                res = jnp.dot(act, ds[half], preferred_element_type=f32).astype(bf16)
                if half == 0:
                    outs[at, :] = res
                else:
                    outs[at, :] = (outs[at, :].astype(f32) + res.astype(f32)).astype(bf16)
                    save(i).start()
                return carry

            step(0, 0, True)
            lax.fori_loop(1, blocks, lambda i, carry: step(i, carry, False), 0)
        for i in range(blocks):
            save(i).wait()

    hbm = pl.BlockSpec(memory_space=pl.ANY)
    return pl.pallas_call(
        body,
        in_specs=[hbm] * 7,
        out_specs=hbm,
        out_shape=jax.ShapeDtypeStruct((rows, width), bf16),
        scratch_shapes=[
            pltpu.VMEM((rows, width), bf16),
            pltpu.VMEM((rows, width), bf16),
            pltpu.VMEM((2, hidden, width), bf16),
            pltpu.VMEM((2, hidden, width), bf16),
            pltpu.VMEM((2, hidden, width), bf16),
            pltpu.SemaphoreType.DMA((blocks,)),
            pltpu.SemaphoreType.DMA((2, 3)),
            pltpu.SemaphoreType.DMA((blocks,)),
        ],
        compiler_params=pltpu.CompilerParams(vmem_limit_bytes=60 * 1024 * 1024),
        cost_estimate=pl.CostEstimate(
            flops=17_700_000_000, bytes_accessed=30_000_000, transcendentals=1_500_000
        ),
        name="experts",
    )(x, *weights)


def routing_tables(ids, gates, experts=64):
    top, rows = ids.shape
    slots = experts * CAP

    def body(ids_ref, gates_ref, spread_ref, mixing_ref):
        expert = lax.broadcasted_iota(jnp.int32, (experts, rows), 0)
        chosen = jnp.zeros((experts, rows), f32)
        gate_of = jnp.zeros((experts, rows), f32)
        for route in range(top):
            named = ids_ref[route : route + 1, :] == expert
            chosen = jnp.where(named, 1.0, chosen)
            gate_of = jnp.where(named, gates_ref[route : route + 1, :], gate_of)
        line = lax.broadcasted_iota(jnp.int32, (rows, rows), 0)
        before = (line < lax.broadcasted_iota(jnp.int32, (rows, rows), 1)).astype(f32).astype(bf16)
        earlier = jnp.dot(chosen.astype(bf16), before, preferred_element_type=f32)
        slot = jnp.where(chosen > 0.0, earlier, -1.0)

        owner = lax.broadcasted_iota(jnp.int32, (slots, experts), 0) // CAP
        owned = owner == lax.broadcasted_iota(jnp.int32, (slots, experts), 1)
        repeat = owned.astype(f32).astype(bf16)
        number = (lax.broadcasted_iota(jnp.int32, (slots, rows), 0) % CAP).astype(f32)
        tall = jnp.dot(repeat, slot.astype(bf16), preferred_element_type=f32)
        spread_ref[...] = (tall == number).astype(f32).astype(bf16)

        owner = lax.broadcasted_iota(jnp.int32, (experts, slots), 1) // CAP
        owned = owner == lax.broadcasted_iota(jnp.int32, (experts, slots), 0)
        repeat = owned.astype(f32).astype(bf16)
        number = (lax.broadcasted_iota(jnp.int32, (rows, slots), 1) % CAP).astype(f32)
        wide = jnp.dot(slot.T.astype(bf16), repeat, preferred_element_type=f32)
        hit = wide == number
        rest = gate_of.T
        for part in range(3):
            now = rest.astype(bf16)
            rest = rest - now.astype(f32)
            weights = jnp.dot(now, repeat, preferred_element_type=f32)
            mixing_ref[part * rows : (part + 1) * rows, :] = jnp.where(hit, weights, 0.0).astype(bf16)

    return pl.pallas_call(
        body,
        out_shape=[
            jax.ShapeDtypeStruct((slots, rows), bf16),
            jax.ShapeDtypeStruct((3 * rows, slots), bf16),
        ],
        name="routing",
    )(ids, gates)


def shards(
    tokens,
    position_of_row,
    request_of_position,
    expert_ids,
    gate_values,
    attn_norm,
    moe_norm,
    w_query,
    w_latent,
    w_key_up,
    w_value_up,
    w_output,
    w_shared_gate,
    w_shared_up,
    w_shared_down,
    w_routed_gate,
    w_routed_up,
    w_routed_down,
):
    own = tokens[0]
    rows, width = own.shape
    here = place_of(0, 0)
    core = lax.axis_index("c")

    spread, mixing = routing_tables(expert_ids[0].T, gate_values[0].T)

    span = w_output.shape[1] // 8
    block_here = lax.axis_index("y") * 2 + core
    columns = lax.dynamic_slice(w_output, (0, block_here * span), (w_output.shape[0], span))
    columns = lax.all_gather(columns, SEQ, axis=0, tiled=True)

    early = (spread, mixing, attn_norm.reshape(1, -1), moe_norm.reshape(1, -1))
    tokens_all, (spread, mixing, attn_gain, moe_gain) = gather_rows(own, early)

    own_half = (w_routed_gate[0].T, w_routed_up[0].T, w_routed_down[0])
    columns, own_half, tokens_all = lax.optimization_barrier((columns, own_half, tokens_all))
    other_half = tuple(swap_cores(w) for w in own_half)
    w_out = lax.all_gather(columns, ("y", "c"), axis=0, tiled=False)

    head_out = attention(
        tokens_all,
        attn_gain,
        w_latent,
        w_query,
        w_key_up,
        w_value_up,
        position_of_row,
        request_of_position,
    )
    head_out, other_half = lax.optimization_barrier((head_out, other_half))
    joined = gather_columns(head_out)

    resid, outgoing = run_dispatch(here, joined, own, w_out, moe_gain, spread)
    outgoing, joined = lax.optimization_barrier((outgoing, joined))
    slots = outgoing.shape[0]
    arrived = lax.all_to_all(
        outgoing.reshape(128, slots // 128, width), ALL, split_axis=0, concat_axis=0, tiled=True
    ).reshape(slots, width)

    shared_part = run_shared(
        joined,
        tokens_all,
        w_out,
        moe_gain,
        w_shared_gate.T,
        w_shared_up.T,
        w_shared_down,
    )
    arrived, _ = lax.optimization_barrier((arrived, shared_part))
    shared_out = lax.psum_scatter(
        shared_part,
        SEQ,
        scatter_dimension=0,
        tiled=True,
    )

    expert_out = run_experts(arrived, own_half + other_half)
    returned = lax.all_to_all(
        expert_out.reshape(128, slots // 128, width), ALL, split_axis=0, concat_axis=0, tiled=True
    ).reshape(slots, width)
    layer_out = run_combine(mixing, returned, resid, shared_out)
    return layer_out.reshape(1, rows, width)


def solution(mesh):
    fine = Mesh(mesh.devices.reshape(2, 4, 2, 4, 2), ALL)
    in_specs = (
        P(EXP, SEQ, None),
        P(EXP, None),
        P(EXP, None),
        P(EXP, SEQ, None),
        P(EXP, SEQ, None),
        P(),
        P(),
        P(None, SEQ),
        P(),
        P(None, SEQ),
        P(None, SEQ),
        P(SEQ, None),
        P(None, SEQ),
        P(None, SEQ),
        P(SEQ, None),
        P(ALL, None, None),
        P(ALL, None, None),
        P(ALL, None, None),
    )
    out_specs = P(EXP, SEQ, None)
    return jax.shard_map(shards, mesh=fine, in_specs=in_specs, out_specs=out_specs, check_vma=False)
```
